32 devices in a mesh: section: 8 (over y, x, core), dp: 4 (over z).
Axes of the slice: x: 2, y: 2, z: 4, core: 2. Of those that a mesh axis runs over, the one named last changes fastest.
Arguments:
- inputs: bfloat16 [4, 8, 128, 4096], P('dp', 'section'), may hold values from -6 to 6
- key_rows: bfloat16 [4, 8, 24, 4096], P('dp', None, None, 'section'), may hold values from -32 to 32
- value_rows: bfloat16 [4, 8, 24, 4096], P('dp', None, None, 'section'), may hold values from -6 to 6
- query_gain: float32 [8, 4096], P('section'), may hold values from 0.1 to 1.9
- cotangent: bfloat16 [4, 8, 128, 4096], P('dp', 'section'), may hold values from -6 to 6
Outputs:
- key_grads: bfloat16 [4, 8, 24, 4096], P('dp', None, None, 'section')
- value_grads: bfloat16 [4, 8, 24, 4096], P('dp', None, None, 'section')
- gain_grads: float32 [8, 4096], P('section')
The draws below stay inside these ranges and needn't reach their ends.
All inputs are finite; a program needn't handle non-finite values.
Results may differ from the reference program's by a relative error of at most 0.008.
Values may be sent and summed in bfloat16 or wider, within the bound.
A program may use at most 64 MiB of HBM per device.

```python
import jax
import jax.numpy as jnp
from jax import lax

D = 4096
HEAD = 64
TOK = 128
SRC = 24
TICKS = 3
LAYERS = 8
DOCS = 4


def draw_inputs(key, part):
    noise_key = jax.random.fold_in(key, 7002)
    drawn = jnp.clip(jax.random.normal(noise_key, (DOCS, LAYERS, TOK, D), jnp.float32), -6.0, 6.0)
    return drawn.astype(jnp.bfloat16)


def draw_key_rows(key, part):
    base = jnp.clip(jax.random.normal(jax.random.fold_in(key, 7011), (DOCS, LAYERS, SRC, D), jnp.float32), -6.0, 6.0)
    return base.astype(jnp.bfloat16)


def block_scale(key, shape, cuts, least, largest):
    loudness = 1.0
    for position, shards_of in cuts:
        steps = jax.random.uniform(jax.random.fold_in(jax.random.fold_in(key, 6), position), (shards_of,), jnp.float32, least / len(cuts), largest / len(cuts))
        loudness = loudness * jnp.repeat(jnp.exp(steps), shape[position] // shards_of).reshape((-1,) + (1,) * (len(shape) - 1 - position))
    return loudness


def scatter_about(key, extent, scale, most, shards=(), dtype=jnp.bfloat16):
    values = jax.random.normal(key, extent, jnp.float32) * scale
    if len(shards) > 0:
        values = block_scale(key, extent, shards, -0.22, 0.18) * values
    return jnp.clip(values, min=-most, max=most).astype(dtype)


def setup_inputs(seed: int = 0) -> dict:
    arg_keys = jax.random.split(jax.random.key(seed), 6)
    inputs = draw_inputs(jax.random.fold_in(arg_keys[5], 71), 0)
    key_rows = draw_key_rows(jax.random.fold_in(arg_keys[5], 71), 0)
    value_rows = scatter_about(arg_keys[2], (DOCS, LAYERS, SRC, D), 1.0, 6.0, ((0, 4), (3, 8)))
    query_gain = jnp.clip(1.0 + 0.18 * jax.random.normal(arg_keys[3], (LAYERS, D), jnp.float32), 0.1, 1.9)
    cotangent = scatter_about(arg_keys[4], (DOCS, LAYERS, TOK, D), 1.0, 6.0, ((0, 4), (1, 8)))
    return {"inputs": inputs, "key_rows": key_rows, "value_rows": value_rows, "query_gain": query_gain, "cotangent": cotangent}


def product(form, left, right):
    return jnp.einsum(form, left.astype(jnp.float32), right.astype(jnp.float32))

def attend_forward(states, gain_row, key_block, value_block):
    floats = states.astype(jnp.float32)
    inverse = lax.rsqrt(lax.optimization_barrier(jnp.mean(floats * floats, axis=-1, keepdims=True)) + 1e-06)
    queries = (floats * inverse * gain_row).astype(jnp.bfloat16)
    tok_rows, width = states.shape
    src_rows = key_block.shape[0]
    heads_count = width // HEAD
    query_heads = queries.reshape(tok_rows, heads_count, HEAD)
    key_heads = key_block.reshape(src_rows, heads_count, HEAD)
    value_heads = value_block.reshape(src_rows, heads_count, HEAD)
    scores = product('shd,thd->hst', key_heads, query_heads) * HEAD ** (-0.5)
    highest = lax.optimization_barrier(jnp.max(scores, axis=1, keepdims=True))
    weights = jnp.exp(scores - highest)
    probs = weights / lax.optimization_barrier(jnp.sum(weights, axis=1, keepdims=True))
    probs_low = probs.astype(jnp.bfloat16)
    mixed = product('hst,shd->thd', probs_low, value_heads).reshape(tok_rows, width)
    produced = (floats + mixed).astype(jnp.bfloat16)
    return (produced, (inverse, queries, probs, probs_low))

def attend_backward(states, gain_row, key_block, value_block, saved, incoming, needed):
    inverse, queries, probs, probs_low = saved
    tok_rows, width = states.shape
    src_rows = key_block.shape[0]
    heads_count = width // HEAD
    query_heads = queries.reshape(tok_rows, heads_count, HEAD)
    key_heads = key_block.reshape(src_rows, heads_count, HEAD)
    value_heads = value_block.reshape(src_rows, heads_count, HEAD)
    grad_heads = incoming.reshape(tok_rows, heads_count, HEAD)
    dprob = product('shd,thd->hst', value_heads, grad_heads)
    dscore = (probs * (dprob - lax.optimization_barrier(jnp.sum(probs * dprob, axis=1, keepdims=True))) * HEAD ** (-0.5)).astype(jnp.bfloat16)
    value_step = product('hst,thd->shd', probs_low, grad_heads).reshape(src_rows, width)
    key_step = product('hst,thd->shd', dscore, query_heads).reshape(src_rows, width)
    dquery = product('hst,shd->thd', dscore, key_heads).reshape(tok_rows, width)
    unit = states.astype(jnp.float32) * inverse
    gain_step = lax.optimization_barrier(jnp.sum(dquery * unit, axis=0))
    if needed:
        scaled = gain_row * dquery
        back = incoming.astype(jnp.float32) + inverse * (scaled - unit * lax.optimization_barrier(jnp.mean(scaled * unit, axis=-1, keepdims=True)))
        back = back.astype(jnp.bfloat16)
    else:
        back = None
    return (back, key_step, value_step, gain_step)

def per_document(inputs_doc, keys_doc, values_doc, cot_doc, query_gain):
    forward = jax.vmap(attend_forward)
    current = inputs_doc
    states = [current]
    for tick_index in range(TICKS - 1):
        produced, unused = forward(current, query_gain, keys_doc, values_doc)
        current = jnp.roll(produced, 1, axis=0)
        states.append(current)
    key_total = jnp.zeros(keys_doc.shape, jnp.float32)
    value_total = jnp.zeros(values_doc.shape, jnp.float32)
    gain_total = jnp.zeros(query_gain.shape, jnp.float32)
    carried = cot_doc
    for tick_index in range(TICKS - 1, -1, -1):
        incoming = jnp.roll(carried, -1, axis=0)
        unused, saved = forward(states[tick_index], query_gain, keys_doc, values_doc)
        needed = tick_index > 0
        backward = jax.vmap(lambda a, b, c, e, f, g: attend_backward(a, b, c, e, f, g, needed))
        carried, key_step, value_step, gain_step = backward(states[tick_index], query_gain, keys_doc, values_doc, saved, incoming)
        key_total = key_total + key_step
        value_total = value_total + value_step
        gain_total = gain_total + gain_step
    return (key_total.astype(jnp.bfloat16), value_total.astype(jnp.bfloat16), gain_total)

def reference(inputs, key_rows, value_rows, query_gain, cotangent):

    def one_doc(packed):
        return per_document(packed[0], packed[1], packed[2], packed[3], query_gain)
    key_grads, value_grads, gain_parts = lax.map(one_doc, (inputs, key_rows, value_rows, cotangent))
    return (key_grads, value_grads, lax.optimization_barrier(jnp.sum(gain_parts, axis=0)))
```

```python
import functools

import jax
import jax.numpy as jnp
from jax import lax
from jax.experimental import pallas as pl
from jax.experimental.pallas import tpu as pltpu
from jax.sharding import PartitionSpec as P

HEAD = 64
TICKS = 3
LANES = 128
MESH = pl.DeviceIdType.MESH
F32 = jnp.float32
BF16 = jnp.bfloat16


def nn(a, b):
    return lax.dot_general(a, b, (((1,), (0,)), ((), ())), preferred_element_type=F32)


def nt(a, b):
    return lax.dot_general(a, b, (((1,), (1,)), ((), ())), preferred_element_type=F32)


def kernel(
    n, ndp, unroll,
    x_ref, ct_ref, k_in, v_in, g_ref,
    kout_ref, vout_ref, gout_ref,
    x_own, k_ref, v_ref,
    xin, cin, gin, stat, kd, vd, kdt, vdt, gt, xs, qs, probs, plow, raws, ds, grads,
    red, inv, ar, ktot, vtot, gsend, gdp,
    x_send, x_recv, c_send, c_recv, g_send, g_recv, st_send, st_recv,
    ar_send, ar_recv, dp_send, dp_recv, loc,
):
    me = lax.axis_index("section")
    doc = lax.axis_index("dp")
    tok, width = x_ref.shape
    src, cols = k_in.shape[1], k_in.shape[2]
    blocks = cols // LANES
    per = LANES // HEAD
    brow = per * src
    scale = HEAD ** (-0.5)

    def peers(body, first=1, last=n):
        def step(j, c):
            body(lax.rem(me + j, n))
            return c
        lax.fori_loop(first, last, step, 0)

    def each(body, first=0, last=n, u=None):
        def step(m, c):
            body(m)
            return c
        lax.fori_loop(first, last, step, 0, unroll=u or min(unroll, last - first))

    half = n // 2
    halves = ((0, half), (half, n))

    def to(p, source, target, send, recv):
        return pltpu.make_async_remote_copy(
            src_ref=source, dst_ref=target, send_sem=send, recv_sem=recv,
            device_id={"section": p}, device_id_type=MESH)

    def others(body):
        def step(j, c):
            place = lax.rem(doc * n + me + j, n * ndp)
            body(lax.div(place, n), lax.rem(place, n))
            return c
        lax.fori_loop(1, n * ndp, step, 0)

    def cut(ref, p):
        return ref.at[:, pl.ds(pl.multiple_of(p * cols, LANES), cols)]

    def x_copy(p, slot):
        return to(p, cut(x_ref, p), xin.at[slot], x_send.at[p], x_recv.at[slot])

    def c_copy(p, slot):
        return to(p, cut(ct_ref, p), cin.at[slot], c_send.at[p], c_recv.at[slot])

    def g_copy(p, slot):
        return to(p, cut(g_ref, p), gin.at[slot], g_send.at[p], g_recv.at[slot])

    def st_copy(p, slot):
        return to(p, stat.at[me], stat.at[slot], st_send.at[p], st_recv.at[slot])

    def ar_copy(a, h, p, slot):
        lo, hi = halves[h]
        return to(p, ar.at[a, me, lo:hi], ar.at[a, slot, lo:hi], ar_send.at[a, h, p], ar_recv.at[a, h, slot])

    def share(a, h):
        peers(lambda p: ar_copy(a, h, p, me).start())

    def dp_copy(q, p, from_doc, slot):
        return pltpu.make_async_remote_copy(
            src_ref=gsend.at[p], dst_ref=gdp.at[from_doc, slot],
            send_sem=dp_send.at[q, p], recv_sem=dp_recv.at[from_doc, slot],
            device_id={"dp": q, "section": p}, device_id_type=MESH)

    barrier = pltpu.get_barrier_semaphore()
    others(lambda q, p: pl.semaphore_signal(
        barrier, inc=1, device_id={"dp": q, "section": p}, device_id_type=MESH))

    own = [
        pltpu.make_async_copy(cut(g_ref, me), gin.at[me], loc.at[0]),
        pltpu.make_async_copy(cut(x_ref, me), xin.at[me], loc.at[1]),
        pltpu.make_async_copy(cut(ct_ref, me), cin.at[me], loc.at[2]),
        pltpu.make_async_copy(x_ref, x_own, loc.at[3]),
        pltpu.make_async_copy(k_in, k_ref, loc.at[4]),
        pltpu.make_async_copy(v_in, v_ref, loc.at[5]),
    ]
    for i in (3, 4, 5, 0, 1, 2):
        own[i].start()

    pl.semaphore_wait(barrier, n * ndp - 1)

    peers(lambda p: x_copy(p, me).start(), 1, 2)
    peers(lambda p: g_copy(p, me).start())
    own[3].wait()
    total = jnp.zeros((tok, LANES), F32)
    for b in range(width // LANES):
        part = x_own[:, b * LANES:(b + 1) * LANES].astype(F32)
        total = total + part * part
    stat[me] = jnp.sum(total.T, axis=0, keepdims=True)
    peers(lambda p: st_copy(p, me).start())
    peers(lambda p: x_copy(p, me).start(), 2)
    first_cut, second_cut = (1 + n) // 4, 1 + (5 * n) // 8
    peers(lambda p: c_copy(p, me).start(), 1, first_cut)
    own[4].wait()
    own[5].wait()

    lane = lax.broadcasted_iota(jnp.int32, (src, LANES), 1)
    sides = [jnp.logical_and(lane >= i * HEAD, lane < (i + 1) * HEAD) for i in range(per)]

    def spread(l):
        for source, plain, turned in ((k_ref, kd, kdt), (v_ref, vd, vdt)):
            rows = source[l].astype(F32)
            for b in range(blocks):
                piece = rows[:, b * LANES:(b + 1) * LANES]
                both = jnp.concatenate([jnp.where(s, piece, 0.0) for s in sides], axis=0)
                plain[l, b] = both.astype(BF16)
                turned[l, b] = both.T.astype(BF16)
        ktot[l] = jnp.zeros((src, cols), F32)
        vtot[l] = jnp.zeros((src, cols), F32)

    each(spread, u=2)

    own[0].wait()
    peers(lambda p: g_copy(p, p).wait_recv())

    def turn_gain(l):
        for b in range(blocks):
            row = gin[l, :, b * LANES:(b + 1) * LANES]
            gt[l, b * LANES:(b + 1) * LANES, :] = jnp.broadcast_to(row, (LANES, LANES)).T

    each(turn_gain, u=2)
    peers(lambda p: st_copy(p, p).wait_recv())

    def fwd(k, m, more):
        l = lax.rem(m + k, n)
        factor = inv[k, m]
        pieces = []
        sums = jnp.zeros((1, tok), F32)
        for b in range(blocks):
            at = slice(b * LANES, (b + 1) * LANES)
            rows = slice(b * brow, (b + 1) * brow)
            xf = xs[k, m, at, :].astype(F32)
            q = (xf * factor * gt[l, at, :]).astype(BF16)
            qs[k, m, at, :] = q
            raw = nn(kd[l, b], q)
            raws[k, m, rows, :] = raw
            s3 = raw.reshape(per, src, tok) * scale
            w = jnp.exp(s3 - jnp.max(s3, axis=1, keepdims=True))
            p = w * (1.0 / jnp.sum(w, axis=1, keepdims=True))
            p = p.reshape(brow, tok)
            probs[k, m, rows, :] = p
            low = p.astype(BF16)
            plow[k, m, rows, :] = low
            if more:
                y = (xf + nn(vdt[l, b], low)).astype(BF16)
                xs[k + 1, m, at, :] = y
                yf = y.astype(F32)
                sums = sums + jnp.sum(yf * yf, axis=0, keepdims=True)
        if more:
            ar[k, me, m] = sums

    def reduced(a, h):
        lo, hi = halves[h]
        peers(lambda p: ar_copy(a, h, p, p).wait_recv())
        total = ar[a, 0, lo:hi]
        for s in range(1, n):
            total = total + ar[a, s, lo:hi]
        return total * (1.0 / width)

    def arrive(j, c):
        m = lax.rem(me + j, n)

        @pl.when(j == 0)
        def _():
            own[1].wait()

        @pl.when(j > 0)
        def _():
            x_copy(m, m).wait_recv()

        inv[0, m] = lax.rsqrt(stat[m] * (1.0 / width) + 1e-6)
        for b in range(blocks):
            at = slice(b * LANES, (b + 1) * LANES)
            xs[0, m, at, :] = xin[m, :, at].T
        fwd(0, m, True)
        return c

    lax.fori_loop(0, n, arrive, 0)
    share(0, 0)
    share(0, 1)
    peers(lambda p: c_copy(p, me).start(), first_cut, second_cut)
    for k in range(1, TICKS):
        for h, (lo, hi) in enumerate(halves):
            inv[k, lo:hi] = lax.rsqrt(reduced(k - 1, h) + 1e-6)
            each(lambda m: fwd(k, m, k + 1 < TICKS), lo, hi)
            if k + 1 < TICKS:
                share(k, h)
        if k == 1:
            peers(lambda p: c_copy(p, me).start(), second_cut, n)

    own[2].wait()

    def arrive_c(p):
        c_copy(p, p).wait_recv()

    def turn_c(m):
        s = lax.rem(m + TICKS, n)
        for b in range(blocks):
            at = slice(b * LANES, (b + 1) * LANES)
            grads[TICKS - 1, m, at, :] = cin[s, :, at].T

    peers(arrive_c)

    def scores_back(k, a, m):
        l = lax.rem(m + k, n)
        sums = jnp.zeros((1, tok), F32)
        for b in range(blocks):
            at = slice(b * LANES, (b + 1) * LANES)
            rows = slice(b * brow, (b + 1) * brow)
            dprob = nn(vd[l, b], grads[k, m, at, :]).reshape(per, src, tok)
            p = probs[k, m, rows, :].reshape(per, src, tok)
            mean = jnp.sum(p * dprob, axis=1, keepdims=True)
            d = (p * (dprob - mean) * scale).reshape(brow, tok).astype(BF16)
            ds[k, m, rows, :] = d
            if a is not None:
                sums = sums + jnp.sum(d.astype(F32) * raws[k, m, rows, :], axis=0, keepdims=True)
        if a is not None:
            ar[a, me, m] = sums

    def picked(r):
        out = r[:src]
        for i in range(1, per):
            out = jnp.where(sides[i], r[i * src:(i + 1) * src], out)
        return out

    def key_step(k, m):
        l = lax.rem(m + k, n)
        for b in range(blocks):
            at = slice(b * LANES, (b + 1) * LANES)
            rows = slice(b * brow, (b + 1) * brow)
            ktot[l, :, at] += picked(nt(ds[k, m, rows, :], qs[k, m, at, :]))

    def value_step(k, m):
        l = lax.rem(m + k, n)
        for b in range(blocks):
            at = slice(b * LANES, (b + 1) * LANES)
            rows = slice(b * brow, (b + 1) * brow)
            vtot[l, :, at] += picked(nt(plow[k, m, rows, :], grads[k, m, at, :]))

    def input_back(k, m):
        l = lax.rem(m + k, n)
        factor = inv[k, m]
        mean = red[m]
        for b in range(blocks):
            at = slice(b * LANES, (b + 1) * LANES)
            rows = slice(b * brow, (b + 1) * brow)
            dq = nn(kdt[l, b], ds[k, m, rows, :])
            u = xs[k, m, at, :].astype(F32) * factor
            back = grads[k, m, at, :].astype(F32) + factor * (gt[l, at, :] * dq - u * mean)
            grads[k - 1, m, at, :] = back.astype(BF16)

    def start_back(m):
        turn_c(m)
        scores_back(TICKS - 1, 2 * TICKS - 3, m)

    for h, (lo, hi) in enumerate(halves):
        each(start_back, lo, hi)
        share(2 * TICKS - 3, h)
    for k in range(TICKS - 1, 0, -1):
        a = TICKS - 1 + k - 1

        def next_back(m):
            input_back(k, m)
            scores_back(k - 1, a - 1 if k > 1 else None, m)

        each(lambda m: key_step(k, m))
        for h, (lo, hi) in enumerate(halves):
            red[lo:hi] = reduced(a, h)
            each(next_back, lo, hi)
            if k > 1:
                share(a - 1, h)

    def last(m):
        key_step(0, m)
        steps = ktot[m]
        kout_ref[m] = steps.astype(BF16)
        gsend[m] = jnp.sum(steps * k_ref[m].astype(F32), axis=0, keepdims=True) / gin[m]

    each(last)
    others(lambda q, p: dp_copy(q, p, doc, me).start())
    gdp[doc, me] = gsend[me]

    each(lambda m: value_step(TICKS - 1, m))
    for k in range(1, TICKS - 1):
        each(lambda m: value_step(k, m))

    def finish(m):
        value_step(0, m)
        vout_ref[m] = vtot[m].astype(BF16)

    each(finish)

    def drain(p):
        x_copy(p, me).wait_send()
        c_copy(p, me).wait_send()
        g_copy(p, me).wait_send()
        st_copy(p, me).wait_send()
        for a in range(2 * (TICKS - 1)):
            for h in range(2):
                ar_copy(a, h, p, me).wait_send()

    peers(drain)
    others(lambda q, p: dp_copy(q, p, q, p).wait_recv())
    others(lambda q, p: dp_copy(q, p, doc, me).wait_send())
    for s in range(n):
        out = gdp[0, s]
        for d in range(1, ndp):
            out = out + gdp[d, s]
        gout_ref[:, s * cols:(s + 1) * cols] = out


def store(keys, values, gains, kout, vout, gout, done):
    copies = [
        pltpu.make_async_copy(keys, kout.at[0], done.at[0]),
        pltpu.make_async_copy(values, vout.at[0], done.at[1]),
        pltpu.make_async_copy(gains, gout, done.at[2]),
    ]
    for copy in copies:
        copy.start()
    for copy in copies:
        copy.wait()


def on_device(inputs, key_rows, value_rows, query_gain, cotangent):
    n = lax.axis_size("section")
    ndp = lax.axis_size("dp")
    tok, width = inputs.shape[2:]
    src, cols = key_rows.shape[2:]
    blocks = cols // LANES
    brow = LANES // HEAD * src
    rows = blocks * brow
    rounds = 2 * (TICKS - 1)
    vmem = pltpu.VMEM
    sem = pltpu.SemaphoreType.DMA
    scratch = [
        vmem((tok, width), BF16), vmem((n, src, cols), BF16), vmem((n, src, cols), BF16),
        vmem((n, tok, cols), BF16), vmem((n, tok, cols), BF16),
        vmem((n, 1, cols), F32), vmem((n, 1, tok), F32),
        vmem((n, blocks, brow, LANES), BF16), vmem((n, blocks, brow, LANES), BF16),
        vmem((n, blocks, LANES, brow), BF16), vmem((n, blocks, LANES, brow), BF16),
        vmem((n, cols, LANES), F32),
        vmem((TICKS, n, cols, tok), BF16), vmem((TICKS, n, cols, tok), BF16),
        vmem((TICKS, n, rows, tok), F32), vmem((TICKS, n, rows, tok), BF16),
        vmem((TICKS, n, rows, tok), F32),
        vmem((TICKS, n, rows, tok), BF16), vmem((TICKS, n, cols, tok), BF16),
        vmem((n, 1, tok), F32), vmem((TICKS, n, 1, tok), F32),
        vmem((rounds, n, n, 1, tok), F32),
        vmem((n, src, cols), F32), vmem((n, src, cols), F32),
        vmem((n, 1, cols), F32), vmem((ndp, n, 1, cols), F32),
        sem((n,)), sem((n,)), sem((n,)), sem((n,)), sem((n,)), sem((n,)), sem((n,)), sem((n,)),
        sem((rounds, 2, n)), sem((rounds, 2, n)), sem((ndp, n)), sem((ndp, n)), sem((6,)),
    ]
    in_vmem = pl.BlockSpec(memory_space=pltpu.VMEM)
    in_place = pl.BlockSpec(memory_space=pl.ANY)
    unroll = 8
    keys, values, gains = pl.pallas_call(
        functools.partial(kernel, n, ndp, unroll),
        out_shape=(
            vmem((n, src, cols), BF16),
            vmem((n, src, cols), BF16),
            vmem((1, width), F32),
        ),
        in_specs=[in_place] * 5,
        out_specs=(in_vmem, in_vmem, in_vmem),
        scratch_shapes=scratch,
        compiler_params=pltpu.CompilerParams(
            collective_id=0, has_side_effects=True, vmem_limit_bytes=60 * 1024 * 1024),
    )(inputs[0, 0], cotangent[0, 0], key_rows[0], value_rows[0], query_gain)
    return pl.pallas_call(
        store,
        out_shape=(
            jax.ShapeDtypeStruct((1, n, src, cols), BF16),
            jax.ShapeDtypeStruct((1, n, src, cols), BF16),
            jax.ShapeDtypeStruct((1, width), F32),
        ),
        in_specs=[in_place] * 3,
        out_specs=(in_place,) * 3,
        scratch_shapes=[sem((3,))],
        compiler_params=pltpu.CompilerParams(vmem_limit_bytes=1024 * 1024),
    )(keys, values, gains)


def solution(mesh):
    return jax.shard_map(
        on_device,
        mesh=mesh,
        in_specs=(
            P("dp", "section", None, None),
            P("dp", None, None, "section"),
            P("dp", None, None, "section"),
            P("section", None),
            P("dp", "section", None, None),
        ),
        out_specs=(
            P("dp", None, None, "section"),
            P("dp", None, None, "section"),
            P("section", None),
        ),
        check_vma=False,
    )
```

```python
import functools

import jax
import jax.numpy as jnp
from jax import lax
from jax.experimental import pallas as pl
from jax.experimental.pallas import tpu as pltpu
from jax.sharding import PartitionSpec as P

HEAD = 64
TICKS = 3
LANES = 128
MESH = pl.DeviceIdType.MESH
F32 = jnp.float32
BF16 = jnp.bfloat16


def nn(a, b):
    return lax.dot_general(a, b, (((1,), (0,)), ((), ())), preferred_element_type=F32)


def nt(a, b):
    return lax.dot_general(a, b, (((1,), (1,)), ((), ())), preferred_element_type=F32)


def kernel(
    n, ndp, unroll,
    x_ref, ct_ref, k_in, v_in, g_ref,
    kout_ref, vout_ref, gout_ref,
    x_own, k_ref, v_ref,
    xin, cin, gin, stat, kd, vd, kdt, vdt, gt, xs, qs, probs, plow, raws, ds, grads,
    wide, e1, e2, inv, ar, br, ktot, vtot, gsend, gdp,
    x_send, x_recv, c_send, c_recv, g_send, g_recv, st_send, st_recv,
    ar_send, ar_recv, br_send, br_recv, dp_send, dp_recv, loc,
):
    me = lax.axis_index("section")
    doc = lax.axis_index("dp")
    tok, width = x_ref.shape
    src, cols = k_in.shape[1], k_in.shape[2]
    blocks = cols // LANES
    per = LANES // HEAD
    brow = per * src
    scale = HEAD ** (-0.5)

    def partner(j):
        p = me
        for b in range(n.bit_length() - 1):
            if (j >> b) & 1:
                p = p + (1 << b) - (2 << b) * lax.rem(lax.div(me, 1 << b), 2)
        return p

    order = sorted(range(n), key=lambda j: ((j >> 1).bit_count(), j & 1, j))
    partners = [partner(j) for j in order]

    def peers(body, first=1, last=n):
        for p in partners[first:last]:
            body(p)

    def each(body, first=0, last=n, u=None):
        def step(m, c):
            body(m)
            return c
        lax.fori_loop(first, last, step, 0, unroll=u or min(unroll, last - first))

    half = n // 2
    halves = ((0, half), (half, n))

    def to(p, source, target, send, recv):
        return pltpu.make_async_remote_copy(
            src_ref=source, dst_ref=target, send_sem=send, recv_sem=recv,
            device_id={"section": p}, device_id_type=MESH)

    def others(body):
        def step(j, c):
            place = lax.rem(doc * n + me + j, n * ndp)
            body(lax.div(place, n), lax.rem(place, n))
            return c
        lax.fori_loop(1, n * ndp, step, 0)

    def cut(ref, p):
        return ref.at[:, pl.ds(pl.multiple_of(p * cols, LANES), cols)]

    def x_copy(p, slot):
        return to(p, cut(x_ref, p), xin.at[slot], x_send.at[p], x_recv.at[slot])

    def c_copy(p, slot):
        return to(p, cut(ct_ref, p), cin.at[slot], c_send.at[p], c_recv.at[slot])

    def g_copy(p, slot):
        return to(p, cut(g_ref, p), gin.at[slot], g_send.at[p], g_recv.at[slot])

    def st_copy(p, slot):
        return to(p, stat.at[me], stat.at[slot], st_send.at[p], st_recv.at[slot])

    def ar_copy(a, h, p, slot):
        lo, hi = halves[h]
        return to(p, ar.at[a, me, lo:hi], ar.at[a, slot, lo:hi], ar_send.at[a, h, p], ar_recv.at[a, h, slot])

    def br_copy(p, slot):
        return to(p, br.at[:, me], br.at[:, slot], br_send.at[p], br_recv.at[slot])

    def share(a, h):
        peers(lambda p: ar_copy(a, h, p, me).start())

    def dp_copy(q, p, from_doc, slot):
        return pltpu.make_async_remote_copy(
            src_ref=gsend.at[p], dst_ref=gdp.at[from_doc, slot],
            send_sem=dp_send.at[q, p], recv_sem=dp_recv.at[from_doc, slot],
            device_id={"dp": q, "section": p}, device_id_type=MESH)

    barrier = pltpu.get_barrier_semaphore()
    others(lambda q, p: pl.semaphore_signal(
        barrier, inc=1, device_id={"dp": q, "section": p}, device_id_type=MESH))

    own = [
        pltpu.make_async_copy(cut(g_ref, me), gin.at[me], loc.at[0]),
        pltpu.make_async_copy(cut(x_ref, me), xin.at[me], loc.at[1]),
        pltpu.make_async_copy(cut(ct_ref, me), cin.at[me], loc.at[2]),
        pltpu.make_async_copy(x_ref, x_own, loc.at[3]),
        pltpu.make_async_copy(k_in, k_ref, loc.at[4]),
        pltpu.make_async_copy(v_in, v_ref, loc.at[5]),
    ]
    for i in (3, 4, 5, 0, 1, 2):
        own[i].start()

    pl.semaphore_wait(barrier, n * ndp - 1)

    peers(lambda p: x_copy(p, me).start(), 1, 2)
    peers(lambda p: g_copy(p, me).start())
    own[3].wait()
    total = jnp.zeros((tok, LANES), F32)
    for b in range(width // LANES):
        part = x_own[:, b * LANES:(b + 1) * LANES].astype(F32)
        total = total + part * part
    stat[me] = jnp.sum(total.T, axis=0, keepdims=True)
    peers(lambda p: st_copy(p, me).start())
    peers(lambda p: x_copy(p, me).start(), 2)
    first_cut, second_cut = n // 2, 3 * n // 4
    peers(lambda p: c_copy(p, me).start(), 1, first_cut)
    own[4].wait()
    own[5].wait()

    lane = lax.broadcasted_iota(jnp.int32, (src, LANES), 1)
    sides = [jnp.logical_and(lane >= i * HEAD, lane < (i + 1) * HEAD) for i in range(per)]

    def spread(l):
        for source, plain, turned in ((k_ref, kd, kdt), (v_ref, vd, vdt)):
            rows = source[l].astype(F32)
            for b in range(blocks):
                piece = rows[:, b * LANES:(b + 1) * LANES]
                both = jnp.concatenate([jnp.where(s, piece, 0.0) for s in sides], axis=0)
                plain[l, b] = both.astype(BF16)
                turned[l, b] = both.T.astype(BF16)
        ktot[l] = jnp.zeros((src, cols), F32)
        vtot[l] = jnp.zeros((src, cols), F32)

    each(spread, u=2)

    own[0].wait()
    peers(lambda p: g_copy(p, p).wait_recv())

    def turn_gain(l):
        for b in range(blocks):
            row = gin[l, :, b * LANES:(b + 1) * LANES]
            gt[l, b * LANES:(b + 1) * LANES, :] = jnp.broadcast_to(row, (LANES, LANES)).T

    each(turn_gain, u=2)
    peers(lambda p: st_copy(p, p).wait_recv())

    def softmax_back(p, dprob):
        dprob = dprob.reshape(per, src, tok)
        mean = jnp.sum(p * dprob, axis=1, keepdims=True)
        return (p * (dprob - mean) * scale).reshape(brow, tok)

    def fwd(k, m, more):
        l = lax.rem(m + k, n)
        factor = inv[k, m]
        pieces = []
        sums = jnp.zeros((1, tok), F32)
        for b in range(blocks):
            at = slice(b * LANES, (b + 1) * LANES)
            rows = slice(b * brow, (b + 1) * brow)
            xf = xs[k, m, at, :].astype(F32)
            q = (xf * factor * gt[l, at, :]).astype(BF16)
            qs[k, m, at, :] = q
            raw = nn(kd[l, b], q)
            raws[k, m, rows, :] = raw
            s3 = raw.reshape(per, src, tok) * scale
            w = jnp.exp(s3 - jnp.max(s3, axis=1, keepdims=True))
            p = w * (1.0 / jnp.sum(w, axis=1, keepdims=True))
            p = p.reshape(brow, tok)
            probs[k, m, rows, :] = p
            low = p.astype(BF16)
            plow[k, m, rows, :] = low
            if more:
                y = (xf + nn(vdt[l, b], low)).astype(BF16)
                xs[k + 1, m, at, :] = y
                yf = y.astype(F32)
                sums = sums + jnp.sum(yf * yf, axis=0, keepdims=True)
            else:
                before = probs[k - 1, m, rows, :].reshape(per, src, tok)
                e = softmax_back(before, nn(vd[lax.rem(m + k - 1, n), b], xs[k, m, at, :]))
                e2[m, rows, :] = e
                sums = sums + jnp.sum(e * raws[k - 1, m, rows, :], axis=0, keepdims=True)
        if more:
            ar[k, me, m] = sums
        else:
            br[2, me, m] = sums

    def reduced(a, h):
        lo, hi = halves[h]
        peers(lambda p: ar_copy(a, h, p, p).wait_recv())
        total = ar[a, 0, lo:hi]
        for s in range(1, n):
            total = total + ar[a, s, lo:hi]
        return total * (1.0 / width)

    def arrive(j):
        m = partners[j]
        if j == 0:
            own[1].wait()
        else:
            x_copy(m, m).wait_recv()

        inv[0, m] = lax.rsqrt(stat[m] * (1.0 / width) + 1e-6)
        for b in range(blocks):
            at = slice(b * LANES, (b + 1) * LANES)
            xs[0, m, at, :] = xin[m, :, at].T
        fwd(0, m, True)

    for j in range(n):
        arrive(j)
    share(0, 0)
    share(0, 1)
    peers(lambda p: c_copy(p, me).start(), first_cut, second_cut)
    for k in range(1, TICKS):
        for h, (lo, hi) in enumerate(halves):
            inv[k, lo:hi] = lax.rsqrt(reduced(k - 1, h) + 1e-6)
            each(lambda m: fwd(k, m, k + 1 < TICKS), lo, hi)
            if k + 1 < TICKS:
                share(k, h)
        if k == 1:
            peers(lambda p: c_copy(p, me).start(), second_cut, n)

    def arrive_c(p):
        c_copy(p, p).wait_recv()

    def turn_c(m):
        s = lax.rem(m + TICKS, n)
        for b in range(blocks):
            at = slice(b * LANES, (b + 1) * LANES)
            grads[TICKS - 1, m, at, :] = cin[s, :, at].T

    def start_back(m):
        k = TICKS - 1
        l = lax.rem(m + k, n)
        earlier = lax.rem(m + k - 1, n)
        factor = inv[k, m]
        sums = jnp.zeros((1, tok), F32)
        ahead = jnp.zeros((1, tok), F32)
        for b in range(blocks):
            at = slice(b * LANES, (b + 1) * LANES)
            rows = slice(b * brow, (b + 1) * brow)
            g = grads[k, m, at, :]
            p = probs[k, m, rows, :].reshape(per, src, tok)
            d = softmax_back(p, nn(vd[l, b], g)).astype(BF16)
            ds[k, m, rows, :] = d
            sums = sums + jnp.sum(d.astype(F32) * raws[k, m, rows, :], axis=0, keepdims=True)
            h = g.astype(F32) + factor * (gt[l, at, :] * nn(kdt[l, b], d))
            wide[m, at, :] = h
            p = probs[k - 1, m, rows, :].reshape(per, src, tok)
            e = softmax_back(p, nn(vd[earlier, b], h.astype(BF16)))
            e1[m, rows, :] = e
            ahead = ahead + jnp.sum(e * raws[k - 1, m, rows, :], axis=0, keepdims=True)
        br[0, me, m] = sums
        br[1, me, m] = ahead

    def picked(r):
        out = r[:src]
        for i in range(1, per):
            out = jnp.where(sides[i], r[i * src:(i + 1) * src], out)
        return out

    def key_step(k, m):
        l = lax.rem(m + k, n)
        for b in range(blocks):
            at = slice(b * LANES, (b + 1) * LANES)
            rows = slice(b * brow, (b + 1) * brow)
            ktot[l, :, at] += picked(nt(ds[k, m, rows, :], qs[k, m, at, :]))

    def value_step(k, m):
        l = lax.rem(m + k, n)
        for b in range(blocks):
            at = slice(b * LANES, (b + 1) * LANES)
            rows = slice(b * brow, (b + 1) * brow)
            vtot[l, :, at] += picked(nt(plow[k, m, rows, :], grads[k, m, at, :]))

    def mean_of(a, m):
        total = br[a, 0, m]
        for j in range(1, n):
            total = total + br[a, j, m]
        return total * (1.0 / width)

    def finish_back(m):
        l1 = lax.rem(m + 1, n)
        late, early = inv[2, m], inv[1, m]
        c = late * late * mean_of(0, m)
        mean = mean_of(1, m) - c * mean_of(2, m)
        for b in range(blocks):
            at = slice(b * LANES, (b + 1) * LANES)
            rows = slice(b * brow, (b + 1) * brow)
            g = (wide[m, at, :] - c * xs[2, m, at, :].astype(F32)).astype(BF16)
            grads[1, m, at, :] = g
            d = (e1[m, rows, :] - c * e2[m, rows, :]).astype(BF16)
            ds[1, m, rows, :] = d
            u = xs[1, m, at, :].astype(F32) * early
            g = g.astype(F32) + early * (gt[l1, at, :] * nn(kdt[l1, b], d) - u * mean)
            g = g.astype(BF16)
            grads[0, m, at, :] = g
            p = probs[0, m, rows, :].reshape(per, src, tok)
            ds[0, m, rows, :] = softmax_back(p, nn(vd[m, b], g)).astype(BF16)

    for j in range(n):
        p = partners[j]
        if j == 0:
            own[2].wait()
        else:
            arrive_c(p)
        m = lax.rem(p + n - TICKS % n, n)
        turn_c(m)
        start_back(m)
    peers(lambda p: br_copy(p, me).start())
    each(lambda m: key_step(2, m))
    each(lambda m: value_step(2, m))
    peers(lambda p: br_copy(p, p).wait_recv())
    each(finish_back)
    each(lambda m: key_step(1, m))

    def last(m):
        key_step(0, m)
        steps = ktot[m]
        kout_ref[m] = steps.astype(BF16)
        gsend[m] = jnp.sum(steps * k_ref[m].astype(F32), axis=0, keepdims=True) / gin[m]

    each(last)
    others(lambda q, p: dp_copy(q, p, doc, me).start())
    gdp[doc, me] = gsend[me]

    each(lambda m: value_step(1, m))

    def finish(m):
        value_step(0, m)
        vout_ref[m] = vtot[m].astype(BF16)

    each(finish)

    def drain(p):
        x_copy(p, me).wait_send()
        c_copy(p, me).wait_send()
        g_copy(p, me).wait_send()
        st_copy(p, me).wait_send()
        br_copy(p, me).wait_send()
        for a in range(TICKS - 1):
            for h in range(2):
                ar_copy(a, h, p, me).wait_send()

    peers(drain)
    others(lambda q, p: dp_copy(q, p, q, p).wait_recv())
    others(lambda q, p: dp_copy(q, p, doc, me).wait_send())
    for s in range(n):
        out = gdp[0, s]
        for d in range(1, ndp):
            out = out + gdp[d, s]
        gout_ref[:, s * cols:(s + 1) * cols] = out


def store(keys, values, gains, kout, vout, gout, done):
    copies = [
        pltpu.make_async_copy(keys, kout.at[0], done.at[0]),
        pltpu.make_async_copy(values, vout.at[0], done.at[1]),
        pltpu.make_async_copy(gains, gout, done.at[2]),
    ]
    for copy in copies:
        copy.start()
    for copy in copies:
        copy.wait()


def on_device(inputs, key_rows, value_rows, query_gain, cotangent):
    n = lax.axis_size("section")
    ndp = lax.axis_size("dp")
    tok, width = inputs.shape[2:]
    src, cols = key_rows.shape[2:]
    blocks = cols // LANES
    brow = LANES // HEAD * src
    rows = blocks * brow
    rounds = TICKS - 1
    vmem = pltpu.VMEM
    sem = pltpu.SemaphoreType.DMA
    scratch = [
        vmem((tok, width), BF16), vmem((n, src, cols), BF16), vmem((n, src, cols), BF16),
        vmem((n, tok, cols), BF16), vmem((n, tok, cols), BF16),
        vmem((n, 1, cols), F32), vmem((n, 1, tok), F32),
        vmem((n, blocks, brow, LANES), BF16), vmem((n, blocks, brow, LANES), BF16),
        vmem((n, blocks, LANES, brow), BF16), vmem((n, blocks, LANES, brow), BF16),
        vmem((n, cols, LANES), F32),
        vmem((TICKS, n, cols, tok), BF16), vmem((TICKS, n, cols, tok), BF16),
        vmem((TICKS, n, rows, tok), F32), vmem((TICKS, n, rows, tok), BF16),
        vmem((TICKS, n, rows, tok), F32),
        vmem((TICKS, n, rows, tok), BF16), vmem((TICKS, n, cols, tok), BF16),
        vmem((n, cols, tok), F32), vmem((n, rows, tok), F32), vmem((n, rows, tok), F32),
        vmem((TICKS, n, 1, tok), F32),
        vmem((rounds, n, n, 1, tok), F32), vmem((3, n, n, 1, tok), F32),
        vmem((n, src, cols), F32), vmem((n, src, cols), F32),
        vmem((n, 1, cols), F32), vmem((ndp, n, 1, cols), F32),
        sem((n,)), sem((n,)), sem((n,)), sem((n,)), sem((n,)), sem((n,)), sem((n,)), sem((n,)),
        sem((rounds, 2, n)), sem((rounds, 2, n)), sem((n,)), sem((n,)), sem((ndp, n)), sem((ndp, n)), sem((6,)),
    ]
    in_vmem = pl.BlockSpec(memory_space=pltpu.VMEM)
    in_place = pl.BlockSpec(memory_space=pl.ANY)
    unroll = 8
    keys, values, gains = pl.pallas_call(
        functools.partial(kernel, n, ndp, unroll),
        out_shape=(
            vmem((n, src, cols), BF16),
            vmem((n, src, cols), BF16),
            vmem((1, width), F32),
        ),
        in_specs=[in_place] * 5,
        out_specs=(in_vmem, in_vmem, in_vmem),
        scratch_shapes=scratch,
        compiler_params=pltpu.CompilerParams(
            collective_id=0, has_side_effects=True, vmem_limit_bytes=60 * 1024 * 1024),
    )(inputs[0, 0], cotangent[0, 0], key_rows[0], value_rows[0], query_gain)
    return pl.pallas_call(
        store,
        out_shape=(
            jax.ShapeDtypeStruct((1, n, src, cols), BF16),
            jax.ShapeDtypeStruct((1, n, src, cols), BF16),
            jax.ShapeDtypeStruct((1, width), F32),
        ),
        in_specs=[in_place] * 3,
        out_specs=(in_place,) * 3,
        scratch_shapes=[sem((3,))],
        compiler_params=pltpu.CompilerParams(vmem_limit_bytes=1024 * 1024),
    )(keys, values, gains)


def solution(mesh):
    return jax.shard_map(
        on_device,
        mesh=mesh,
        in_specs=(
            P("dp", "section", None, None),
            P("dp", None, None, "section"),
            P("dp", None, None, "section"),
            P("section", None),
            P("dp", "section", None, None),
        ),
        out_specs=(
            P("dp", None, None, "section"),
            P("dp", None, None, "section"),
            P("section", None),
        ),
        check_vma=False,
    )
```

```python
import functools

import jax
import jax.numpy as jnp
from jax import lax
from jax.experimental import pallas as pl
from jax.experimental.pallas import tpu as pltpu
from jax.sharding import PartitionSpec as P

HEAD = 64
TICKS = 3
LANES = 128
MESH = pl.DeviceIdType.MESH
F32 = jnp.float32
BF16 = jnp.bfloat16


def nn(a, b):
    return lax.dot_general(a, b, (((1,), (0,)), ((), ())), preferred_element_type=F32)


def nt(a, b):
    return lax.dot_general(a, b, (((1,), (1,)), ((), ())), preferred_element_type=F32)


def kernel(
    n, ndp, unroll,
    x_ref, ct_ref, k_in, v_in, g_ref,
    kout_ref, vout_ref, gout_ref,
    x_own, k_ref, v_ref,
    xin, cin, gin, stat, kd, vd, kdt, vdt, gt, xs, qs, probs, plow, raws, ds, grads,
    wide, e1, e2, inv, ar, br, ktot, vtot, gsend, gdp,
    x_send, x_recv, c_send, c_recv, g_send, g_recv, st_send, st_recv,
    ar_send, ar_recv, br_send, br_recv, dp_send, dp_recv, loc,
):
    me = lax.axis_index("section")
    doc = lax.axis_index("dp")
    tok, width = x_ref.shape
    src, cols = k_in.shape[1], k_in.shape[2]
    blocks = cols // LANES
    per = LANES // HEAD
    brow = per * src
    scale = HEAD ** (-0.5)

    def partner(j):
        p = me
        for b in range(n.bit_length() - 1):
            if (j >> b) & 1:
                p = p + (1 << b) - (2 << b) * lax.rem(lax.div(me, 1 << b), 2)
        return p

    order = sorted(range(n), key=lambda j: ((j >> 1).bit_count(), j & 1, j))
    partners = [partner(j) for j in order]

    def peers(body, first=1, last=n):
        for p in partners[first:last]:
            body(p)

    def each(body, first=0, last=n, u=None):
        def step(m, c):
            body(m)
            return c
        lax.fori_loop(first, last, step, 0, unroll=u or min(unroll, last - first))

    half = n // 2
    halves = ((0, half), (half, n))

    def to(p, source, target, send, recv):
        return pltpu.make_async_remote_copy(
            src_ref=source, dst_ref=target, send_sem=send, recv_sem=recv,
            device_id={"section": p}, device_id_type=MESH)

    def others(body):
        def step(j, c):
            place = lax.rem(doc * n + me + j, n * ndp)
            body(lax.div(place, n), lax.rem(place, n))
            return c
        lax.fori_loop(1, n * ndp, step, 0)

    def cut(ref, p):
        return ref.at[:, pl.ds(pl.multiple_of(p * cols, LANES), cols)]

    def x_copy(p, slot):
        return to(p, cut(x_ref, p), xin.at[slot], x_send.at[p], x_recv.at[slot])

    def c_copy(p, slot, part):
        rows = pl.ds(part * (tok // 2), tok // 2)
        source = ct_ref.at[rows, pl.ds(pl.multiple_of(p * cols, LANES), cols)]
        return to(p, source, cin.at[slot, rows], c_send.at[part, p], c_recv.at[part, slot])

    units = []
    for j in range(1, n - 1, 2):
        units += [(j, 0), (j + 1, 0), (j, 1), (j + 1, 1)]
    units = [(1, 0), (1, 1)] + [(j + 1, part) for j, part in units]
    units = [(j, part) for j, part in units if j < n]

    def c_send_units(lo, hi):
        for j, part in units[lo:hi]:
            c_copy(partners[j], me, part).start()

    def g_copy(p, slot):
        return to(p, cut(g_ref, p), gin.at[slot], g_send.at[p], g_recv.at[slot])

    def st_copy(p, slot):
        return to(p, stat.at[me], stat.at[slot], st_send.at[p], st_recv.at[slot])

    def ar_copy(a, h, p, slot):
        lo, hi = halves[h]
        return to(p, ar.at[a, me, lo:hi], ar.at[a, slot, lo:hi], ar_send.at[a, h, p], ar_recv.at[a, h, slot])

    def br_copy(p, slot):
        return to(p, br.at[:, me], br.at[:, slot], br_send.at[p], br_recv.at[slot])

    def share(a, h):
        peers(lambda p: ar_copy(a, h, p, me).start())

    def dp_copy(q, p, from_doc, slot):
        return pltpu.make_async_remote_copy(
            src_ref=gsend.at[p], dst_ref=gdp.at[from_doc, slot],
            send_sem=dp_send, recv_sem=dp_recv,
            device_id={"dp": q, "section": p}, device_id_type=MESH)

    barrier = pltpu.get_barrier_semaphore()
    others(lambda q, p: pl.semaphore_signal(
        barrier, inc=1, device_id={"dp": q, "section": p}, device_id_type=MESH))

    own = [
        pltpu.make_async_copy(cut(g_ref, me), gin.at[me], loc.at[0]),
        pltpu.make_async_copy(cut(x_ref, me), xin.at[me], loc.at[1]),
        pltpu.make_async_copy(cut(ct_ref, me), cin.at[me], loc.at[2]),
        pltpu.make_async_copy(x_ref, x_own, loc.at[3]),
        pltpu.make_async_copy(k_in, k_ref, loc.at[4]),
        pltpu.make_async_copy(v_in, v_ref, loc.at[5]),
    ]
    for i in (3, 4, 5, 0, 1, 2):
        own[i].start()

    pl.semaphore_wait(barrier, n * ndp - 1)

    peers(lambda p: g_copy(p, me).start())
    peers(lambda p: x_copy(p, me).start(), 1, n // 2)
    own[3].wait()
    total = jnp.zeros((tok, LANES), F32)
    for b in range(width // LANES):
        part = x_own[:, b * LANES:(b + 1) * LANES].astype(F32)
        total = total + part * part
    stat[me] = jnp.sum(total.T, axis=0, keepdims=True)
    peers(lambda p: st_copy(p, me).start())
    peers(lambda p: x_copy(p, me).start(), n // 2)
    first_cut, second_cut = n - 2, n + 2
    c_send_units(0, first_cut)
    own[4].wait()
    own[5].wait()

    lane = lax.broadcasted_iota(jnp.int32, (src, LANES), 1)
    sides = [jnp.logical_and(lane >= i * HEAD, lane < (i + 1) * HEAD) for i in range(per)]

    def spread(l):
        for source, plain, turned in ((k_ref, kd, kdt), (v_ref, vd, vdt)):
            rows = source[l].astype(F32)
            for b in range(blocks):
                piece = rows[:, b * LANES:(b + 1) * LANES]
                both = jnp.concatenate([jnp.where(s, piece, 0.0) for s in sides], axis=0)
                plain[l, b] = both.astype(BF16)
                turned[l, b] = both.T.astype(BF16)
        ktot[l] = jnp.zeros((src, cols), F32)
        vtot[l] = jnp.zeros((src, cols), F32)

    each(spread, u=2)

    own[0].wait()
    peers(lambda p: g_copy(p, p).wait_recv())

    def turn_gain(l):
        for b in range(blocks):
            row = gin[l, :, b * LANES:(b + 1) * LANES]
            gt[l, b * LANES:(b + 1) * LANES, :] = jnp.broadcast_to(row, (LANES, LANES)).T

    each(turn_gain, u=2)
    peers(lambda p: st_copy(p, p).wait_recv())

    def softmax_back(p, dprob):
        dprob = dprob.reshape(per, src, tok)
        mean = jnp.sum(p * dprob, axis=1, keepdims=True)
        return (p * (dprob - mean) * scale).reshape(brow, tok)

    def fwd(k, m, more):
        l = lax.rem(m + k, n)
        factor = inv[k, m]
        pieces = []
        sums = jnp.zeros((1, tok), F32)
        for b in range(blocks):
            at = slice(b * LANES, (b + 1) * LANES)
            rows = slice(b * brow, (b + 1) * brow)
            xf = xs[k, m, at, :].astype(F32)
            q = (xf * factor * gt[l, at, :]).astype(BF16)
            qs[k, m, at, :] = q
            raw = nn(kd[l, b], q)
            raws[k, m, rows, :] = raw
            s3 = raw.reshape(per, src, tok) * scale
            w = jnp.exp(s3 - jnp.max(s3, axis=1, keepdims=True))
            p = w * (1.0 / jnp.sum(w, axis=1, keepdims=True))
            p = p.reshape(brow, tok)
            probs[k, m, rows, :] = p
            low = p.astype(BF16)
            plow[k, m, rows, :] = low
            if more:
                y = (xf + nn(vdt[l, b], low)).astype(BF16)
                xs[k + 1, m, at, :] = y
                yf = y.astype(F32)
                sums = sums + jnp.sum(yf * yf, axis=0, keepdims=True)
            else:
                before = probs[k - 1, m, rows, :].reshape(per, src, tok)
                e = softmax_back(before, nn(vd[lax.rem(m + k - 1, n), b], xs[k, m, at, :]))
                e2[m, rows, :] = e
                sums = sums + jnp.sum(e * raws[k - 1, m, rows, :], axis=0, keepdims=True)
        if more:
            ar[k, me, m] = sums
        else:
            br[2, me, m] = sums

    def reduced(a, h):
        lo, hi = halves[h]
        peers(lambda p: ar_copy(a, h, p, p).wait_recv())
        total = ar[a, 0, lo:hi]
        for s in range(1, n):
            total = total + ar[a, s, lo:hi]
        return total * (1.0 / width)

    def arrive(j):
        m = partners[j]
        if j == 0:
            own[1].wait()
        else:
            x_copy(m, m).wait_recv()

        inv[0, m] = lax.rsqrt(stat[m] * (1.0 / width) + 1e-6)
        for b in range(blocks):
            at = slice(b * LANES, (b + 1) * LANES)
            xs[0, m, at, :] = xin[m, :, at].T
        fwd(0, m, True)

    for j in range(n):
        arrive(j)
    share(0, 0)
    share(0, 1)
    c_send_units(first_cut, second_cut)
    for k in range(1, TICKS):
        for h, (lo, hi) in enumerate(halves):
            inv[k, lo:hi] = lax.rsqrt(reduced(k - 1, h) + 1e-6)
            each(lambda m: fwd(k, m, k + 1 < TICKS), lo, hi)
            if k + 1 < TICKS:
                share(k, h)
        if k == 1:
            c_send_units(second_cut, len(units))

    def arrive_c(p):
        c_copy(p, p, 0).wait_recv()
        c_copy(p, p, 1).wait_recv()

    def turn_c(m):
        s = lax.rem(m + TICKS, n)
        for b in range(blocks):
            at = slice(b * LANES, (b + 1) * LANES)
            grads[TICKS - 1, m, at, :] = cin[s, :, at].T

    def start_back(m):
        k = TICKS - 1
        l = lax.rem(m + k, n)
        earlier = lax.rem(m + k - 1, n)
        factor = inv[k, m]
        sums = jnp.zeros((1, tok), F32)
        ahead = jnp.zeros((1, tok), F32)
        for b in range(blocks):
            at = slice(b * LANES, (b + 1) * LANES)
            rows = slice(b * brow, (b + 1) * brow)
            g = grads[k, m, at, :]
            p = probs[k, m, rows, :].reshape(per, src, tok)
            d = softmax_back(p, nn(vd[l, b], g)).astype(BF16)
            ds[k, m, rows, :] = d
            sums = sums + jnp.sum(d.astype(F32) * raws[k, m, rows, :], axis=0, keepdims=True)
            h = g.astype(F32) + factor * (gt[l, at, :] * nn(kdt[l, b], d))
            wide[m, at, :] = h
            p = probs[k - 1, m, rows, :].reshape(per, src, tok)
            e = softmax_back(p, nn(vd[earlier, b], h.astype(BF16)))
            e1[m, rows, :] = e
            ahead = ahead + jnp.sum(e * raws[k - 1, m, rows, :], axis=0, keepdims=True)
        br[0, me, m] = sums
        br[1, me, m] = ahead

    def picked(r):
        out = r[:src]
        for i in range(1, per):
            out = jnp.where(sides[i], r[i * src:(i + 1) * src], out)
        return out

    def key_step(k, m):
        l = lax.rem(m + k, n)
        for b in range(blocks):
            at = slice(b * LANES, (b + 1) * LANES)
            rows = slice(b * brow, (b + 1) * brow)
            ktot[l, :, at] += picked(nt(ds[k, m, rows, :], qs[k, m, at, :]))

    def pair(ref, l, rows):
        return jnp.concatenate(
            [ref[1, lax.rem(l + n - 1, n), rows, :], ref[0, l, rows, :]], axis=1)

    def paired(left, right, l):
        out = []
        for b in range(blocks):
            at = slice(b * LANES, (b + 1) * LANES)
            rows = slice(b * brow, (b + 1) * brow)
            out.append(picked(nt(pair(left, l, rows), pair(right, l, at))))
        return jnp.concatenate(out, axis=1)

    def value_step(k, m):
        l = lax.rem(m + k, n)
        for b in range(blocks):
            at = slice(b * LANES, (b + 1) * LANES)
            rows = slice(b * brow, (b + 1) * brow)
            vtot[l, :, at] += picked(nt(plow[k, m, rows, :], grads[k, m, at, :]))

    def mean_of(a, m):
        total = br[a, 0, m]
        for j in range(1, n):
            total = total + br[a, j, m]
        return total * (1.0 / width)

    def finish_back(m):
        l1 = lax.rem(m + 1, n)
        late, early = inv[2, m], inv[1, m]
        c = late * late * mean_of(0, m)
        mean = mean_of(1, m) - c * mean_of(2, m)
        for b in range(blocks):
            at = slice(b * LANES, (b + 1) * LANES)
            rows = slice(b * brow, (b + 1) * brow)
            g = (wide[m, at, :] - c * xs[2, m, at, :].astype(F32)).astype(BF16)
            grads[1, m, at, :] = g
            d = (e1[m, rows, :] - c * e2[m, rows, :]).astype(BF16)
            ds[1, m, rows, :] = d
            u = xs[1, m, at, :].astype(F32) * early
            g = g.astype(F32) + early * (gt[l1, at, :] * nn(kdt[l1, b], d) - u * mean)
            g = g.astype(BF16)
            grads[0, m, at, :] = g
            p = probs[0, m, rows, :].reshape(per, src, tok)
            ds[0, m, rows, :] = softmax_back(p, nn(vd[m, b], g)).astype(BF16)

    for j in range(n):
        p = partners[j]
        if j == 0:
            own[2].wait()
        else:
            arrive_c(p)
        m = lax.rem(p + n - TICKS % n, n)
        turn_c(m)
        start_back(m)
    peers(lambda p: br_copy(p, me).start())
    each(lambda m: key_step(2, m))
    each(lambda m: value_step(2, m))
    peers(lambda p: br_copy(p, p).wait_recv())
    each(finish_back)

    def last(l):
        steps = ktot[l] + paired(ds, qs, l)
        kout_ref[l] = steps.astype(BF16)
        gsend[l] = jnp.sum(steps * k_ref[l].astype(F32), axis=0, keepdims=True) / gin[l]

    each(last)
    own_gain = pltpu.make_async_copy(gsend.at[me], gdp.at[doc, me], dp_recv)
    others(lambda q, p: dp_copy(q, p, doc, me).start())
    own_gain.start()

    def finish(l):
        vout_ref[l] = (vtot[l] + paired(plow, grads, l)).astype(BF16)

    each(finish)

    def drain(p):
        x_copy(p, me).wait_send()
        c_copy(p, me, 0).wait_send()
        c_copy(p, me, 1).wait_send()
        g_copy(p, me).wait_send()
        st_copy(p, me).wait_send()
        br_copy(p, me).wait_send()
        for a in range(TICKS - 1):
            for h in range(2):
                ar_copy(a, h, p, me).wait_send()

    peers(drain)
    pltpu.make_async_copy(gdp, gdp, dp_recv).wait()
    for d in range(ndp - 1):
        pltpu.make_async_copy(gdp.at[d], gdp.at[d], dp_send).wait()
    pltpu.make_async_copy(gdp.at[0, 1:], gdp.at[0, 1:], dp_send).wait()
    for s in range(n):
        out = gdp[0, s]
        for d in range(1, ndp):
            out = out + gdp[d, s]
        gout_ref[:, s * cols:(s + 1) * cols] = out


def store(keys, values, gains, kout, vout, gout, done):
    copies = [
        pltpu.make_async_copy(keys, kout.at[0], done.at[0]),
        pltpu.make_async_copy(values, vout.at[0], done.at[1]),
        pltpu.make_async_copy(gains, gout, done.at[2]),
    ]
    for copy in copies:
        copy.start()
    for copy in copies:
        copy.wait()


def on_device(inputs, key_rows, value_rows, query_gain, cotangent):
    n = lax.axis_size("section")
    ndp = lax.axis_size("dp")
    tok, width = inputs.shape[2:]
    src, cols = key_rows.shape[2:]
    blocks = cols // LANES
    brow = LANES // HEAD * src
    rows = blocks * brow
    rounds = TICKS - 1
    vmem = pltpu.VMEM
    sem = pltpu.SemaphoreType.DMA
    scratch = [
        vmem((tok, width), BF16), vmem((n, src, cols), BF16), vmem((n, src, cols), BF16),
        vmem((n, tok, cols), BF16), vmem((n, tok, cols), BF16),
        vmem((n, 1, cols), F32), vmem((n, 1, tok), F32),
        vmem((n, blocks, brow, LANES), BF16), vmem((n, blocks, brow, LANES), BF16),
        vmem((n, blocks, LANES, brow), BF16), vmem((n, blocks, LANES, brow), BF16),
        vmem((n, cols, LANES), F32),
        vmem((TICKS, n, cols, tok), BF16), vmem((TICKS, n, cols, tok), BF16),
        vmem((TICKS, n, rows, tok), F32), vmem((TICKS, n, rows, tok), BF16),
        vmem((TICKS, n, rows, tok), F32),
        vmem((TICKS, n, rows, tok), BF16), vmem((TICKS, n, cols, tok), BF16),
        vmem((n, cols, tok), F32), vmem((n, rows, tok), F32), vmem((n, rows, tok), F32),
        vmem((TICKS, n, 1, tok), F32),
        vmem((rounds, n, n, 1, tok), F32), vmem((3, n, n, 1, tok), F32),
        vmem((n, src, cols), F32), vmem((n, src, cols), F32),
        vmem((n, 1, cols), F32), vmem((ndp, n, 1, cols), F32),
        sem((n,)), sem((n,)), sem((2, n)), sem((2, n)), sem((n,)), sem((n,)), sem((n,)), sem((n,)),
        sem((rounds, 2, n)), sem((rounds, 2, n)), sem((n,)), sem((n,)), sem(()), sem(()), sem((6,)),
    ]
    in_vmem = pl.BlockSpec(memory_space=pltpu.VMEM)
    in_place = pl.BlockSpec(memory_space=pl.ANY)
    unroll = 8
    keys, values, gains = pl.pallas_call(
        functools.partial(kernel, n, ndp, unroll),
        out_shape=(
            vmem((n, src, cols), BF16),
            vmem((n, src, cols), BF16),
            vmem((1, width), F32),
        ),
        in_specs=[in_place] * 5,
        out_specs=(in_vmem, in_vmem, in_vmem),
        scratch_shapes=scratch,
        compiler_params=pltpu.CompilerParams(
            collective_id=0, has_side_effects=True, vmem_limit_bytes=60 * 1024 * 1024),
    )(inputs[0, 0], cotangent[0, 0], key_rows[0], value_rows[0], query_gain)
    return pl.pallas_call(
        store,
        out_shape=(
            jax.ShapeDtypeStruct((1, n, src, cols), BF16),
            jax.ShapeDtypeStruct((1, n, src, cols), BF16),
            jax.ShapeDtypeStruct((1, width), F32),
        ),
        in_specs=[in_place] * 3,
        out_specs=(in_place,) * 3,
        scratch_shapes=[sem((3,))],
        compiler_params=pltpu.CompilerParams(vmem_limit_bytes=1024 * 1024),
    )(keys, values, gains)


def solution(mesh):
    return jax.shard_map(
        on_device,
        mesh=mesh,
        in_specs=(
            P("dp", "section", None, None),
            P("dp", None, None, "section"),
            P("dp", None, None, "section"),
            P("section", None),
            P("dp", "section", None, None),
        ),
        out_specs=(
            P("dp", None, None, "section"),
            P("dp", None, None, "section"),
            P("section", None),
        ),
        check_vma=False,
    )
```

```python
import functools

import jax
import jax.numpy as jnp
from jax import lax
from jax.experimental import pallas as pl
from jax.experimental.pallas import tpu as pltpu
from jax.sharding import PartitionSpec as P

HEAD = 64
TICKS = 3
LANES = 128
MESH = pl.DeviceIdType.MESH
F32 = jnp.float32
BF16 = jnp.bfloat16


def nn(a, b):
    return lax.dot_general(a, b, (((1,), (0,)), ((), ())), preferred_element_type=F32)


def nt(a, b):
    return lax.dot_general(a, b, (((1,), (1,)), ((), ())), preferred_element_type=F32)


def kernel(
    n, ndp, unroll,
    x_ref, ct_ref, k_in, v_in, g_ref,
    kout_ref, vout_ref, gout_ref,
    x_own, k_ref, v_ref,
    xin, cin, gin, stat, kd, vd, kdt, vdt, gt, xs, qs, probs, plow, raws, ds, grads,
    wide, e1, e2, inv, ar, br, ktot, vtot, gsend, gdp,
    x_send, x_recv, c_send, c_recv, g_send, g_recv, st_send, st_recv,
    ar_send, ar_recv, br_send, br_recv, dp_send, dp_recv, loc,
):
    me = lax.axis_index("section")
    doc = lax.axis_index("dp")
    tok, width = x_ref.shape
    src, cols = k_in.shape[1], k_in.shape[2]
    blocks = cols // LANES
    per = LANES // HEAD
    brow = per * src
    scale = HEAD ** (-0.5)

    share_of = 2 if blocks % 2 == 0 else 1
    groups = [tuple(range(b, b + share_of)) for b in range(0, blocks, share_of)]

    singles = [(b,) for b in range(blocks)]

    def span(b):
        return slice(b * LANES, (b + 1) * LANES), slice(b * brow, (b + 1) * brow)

    def products(table, l, group, rights):
        left = jnp.concatenate([table[l, b] for b in group], axis=0)
        out = nn(left, jnp.concatenate(rights, axis=1))
        return [out[i * brow:(i + 1) * brow, i * tok:(i + 1) * tok] for i in range(len(group))]

    def partner(j):
        p = me
        for b in range(n.bit_length() - 1):
            if (j >> b) & 1:
                p = p + (1 << b) - (2 << b) * lax.rem(lax.div(me, 1 << b), 2)
        return p

    order = sorted(range(n), key=lambda j: ((j >> 1).bit_count(), j & 1, j))
    partners = [partner(j) for j in order]

    def across(p):
        v = 0
        for b in range(n.bit_length() - 1):
            v = v + (1 << b) * lax.rem(lax.div(me, 1 << b) + lax.div(p, 1 << b), 2)
        return v

    def peers(body, first=1, last=n):
        for p in partners[first:last]:
            body(p)

    def each(body, first=0, last=n, u=None):
        def step(m, c):
            body(m)
            return c
        lax.fori_loop(first, last, step, 0, unroll=u or min(unroll, last - first))

    half = n // 2
    halves = ((0, half), (half, n))

    def to(p, source, target, send, recv):
        return pltpu.make_async_remote_copy(
            src_ref=source, dst_ref=target, send_sem=send, recv_sem=recv,
            device_id={"section": p}, device_id_type=MESH)

    def others(body):
        def step(j, c):
            place = lax.rem(doc * n + me + j, n * ndp)
            body(lax.div(place, n), lax.rem(place, n))
            return c
        lax.fori_loop(1, n * ndp, step, 0)

    def cut(ref, p):
        return ref.at[:, pl.ds(pl.multiple_of(p * cols, LANES), cols)]

    def x_copy(p, slot):
        return to(p, cut(x_ref, p), xin.at[slot], x_send.at[p], x_recv.at[slot])

    def c_copy(p, slot, part):
        rows = pl.ds(part * (tok // 2), tok // 2)
        source = ct_ref.at[rows, pl.ds(pl.multiple_of(p * cols, LANES), cols)]
        return to(p, source, cin.at[slot, rows], c_send.at[part, p], c_recv.at[part, slot])

    units = [(1, 0), (1, 1)]
    for j in range(2, n - 2, 2):
        units += [(j, 0), (j + 1, 0), (j, 1), (j + 1, 1)]
    units += [(j, part) for j in (n - 2, n - 1) for part in (0, 1)]

    def c_send_units(lo, hi):
        for j, part in units[lo:hi]:
            c_copy(partners[j], me, part).start()

    def g_copy(p, slot):
        return to(p, cut(g_ref, p), gin.at[slot], g_send.at[p], g_recv.at[slot])

    def st_copy(p, slot):
        return to(p, stat.at[me], stat.at[slot], st_send.at[p], st_recv.at[slot])

    def ar_copy(a, h, p, slot):
        lo, hi = halves[h]
        return to(p, ar.at[a, me, lo:hi], ar.at[a, slot, lo:hi], ar_send.at[a, h, p], ar_recv.at[a, h, slot])

    def br_copy(p, slot):
        return to(p, br.at[:, me], br.at[:, slot], br_send.at[p], br_recv.at[slot])

    def share(a, h):
        peers(lambda p: ar_copy(a, h, p, me).start())

    def dp_copy(q, p, from_doc, slot):
        return pltpu.make_async_remote_copy(
            src_ref=gsend.at[p], dst_ref=gdp.at[from_doc, slot],
            send_sem=dp_send, recv_sem=dp_recv,
            device_id={"dp": q, "section": p}, device_id_type=MESH)

    barrier = pltpu.get_barrier_semaphore()
    others(lambda q, p: pl.semaphore_signal(
        barrier, inc=1, device_id={"dp": q, "section": p}, device_id_type=MESH))

    own = [
        pltpu.make_async_copy(cut(g_ref, me), gin.at[me], loc.at[0]),
        pltpu.make_async_copy(cut(x_ref, me), xin.at[me], loc.at[1]),
        pltpu.make_async_copy(cut(ct_ref, me), cin.at[me], loc.at[2]),
        pltpu.make_async_copy(x_ref, x_own, loc.at[3]),
        pltpu.make_async_copy(k_in, k_ref, loc.at[4]),
        pltpu.make_async_copy(v_in, v_ref, loc.at[5]),
    ]
    for i in (3, 4, 5, 0, 1, 2):
        own[i].start()

    pl.semaphore_wait(barrier, n * ndp - 1)

    peers(lambda p: g_copy(p, me).start())
    peers(lambda p: x_copy(p, me).start(), 1, n // 2)
    own[3].wait()
    total = jnp.zeros((tok, LANES), F32)
    for b in range(width // LANES):
        part = x_own[:, b * LANES:(b + 1) * LANES].astype(F32)
        total = total + part * part
    stat[me] = jnp.sum(total.T, axis=0, keepdims=True)
    peers(lambda p: st_copy(p, me).start())
    peers(lambda p: x_copy(p, me).start(), n // 2)
    first_cut, second_cut = n - 2, n + 2
    c_send_units(0, first_cut)
    own[4].wait()
    own[5].wait()

    lane = lax.broadcasted_iota(jnp.int32, (src, LANES), 1)
    sides = [jnp.logical_and(lane >= i * HEAD, lane < (i + 1) * HEAD) for i in range(per)]

    def spread(l):
        for source, plain, turned in ((k_ref, kd, kdt), (v_ref, vd, vdt)):
            rows = source[l].astype(F32)
            for b in range(blocks):
                piece = rows[:, b * LANES:(b + 1) * LANES]
                both = jnp.concatenate([jnp.where(s, piece, 0.0) for s in sides], axis=0)
                plain[l, b] = both.astype(BF16)
                turned[l, b] = both.T.astype(BF16)

    each(spread, u=2)

    own[0].wait()
    peers(lambda p: g_copy(p, p).wait_recv())

    def turn_gain(l):
        for b in range(blocks):
            row = gin[l, :, b * LANES:(b + 1) * LANES]
            gt[l, b * LANES:(b + 1) * LANES, :] = jnp.broadcast_to(row, (LANES, LANES)).T

    each(turn_gain, u=2)
    peers(lambda p: st_copy(p, p).wait_recv())

    def softmax_back(p, dprob):
        dprob = dprob.reshape(per, src, tok)
        mean = jnp.sum(p * dprob, axis=1, keepdims=True)
        return (p * (dprob - mean) * scale).reshape(brow, tok)

    def fwd(k, m, more, states=None):
        l = lax.rem(m + k, n)
        factor = inv[k, m]
        pieces = []
        sums = jnp.zeros((1, tok), F32)
        for group in singles:
            xfs, queries = [], []
            for b in group:
                at, _ = span(b)
                xf = (xs[k, m, at, :] if states is None else states[b]).astype(F32)
                q = (xf * factor * gt[l, at, :]).astype(BF16)
                qs[k, m, at, :] = q
                xfs.append(xf)
                queries.append(q)
            scores = products(kd, l, group, queries)
            for b, xf, raw in zip(group, xfs, scores):
                at, rows = span(b)
                raws[k, m, rows, :] = raw
                s3 = raw.reshape(per, src, tok) * scale
                w = jnp.exp(s3 - jnp.max(s3, axis=1, keepdims=True))
                p = w * (1.0 / jnp.sum(w, axis=1, keepdims=True))
                p = p.reshape(brow, tok)
                probs[k, m, rows, :] = p
                low = p.astype(BF16)
                plow[k, m, rows, :] = low
                if more:
                    y = (xf + nn(vdt[l, b], low)).astype(BF16)
                    xs[k + 1, m, at, :] = y
                    yf = y.astype(F32)
                    sums = sums + jnp.sum(yf * yf, axis=0, keepdims=True)
        if more:
            ar[k, me, m] = sums

    def response(m):
        sums = jnp.zeros((1, tok), F32)
        for group in groups:
            out = products(vd, lax.rem(m + 1, n), group, [xs[2, m, span(b)[0], :] for b in group])
            for b, dprob in zip(group, out):
                _, rows = span(b)
                e = softmax_back(probs[1, m, rows, :].reshape(per, src, tok), dprob)
                e2[m, rows, :] = e
                sums = sums + jnp.sum(e * raws[1, m, rows, :], axis=0, keepdims=True)
        br[2, me, m] = sums

    def reduced(a, h):
        lo, hi = halves[h]
        peers(lambda p: ar_copy(a, h, p, p).wait_recv())
        total = ar[a, 0, lo:hi]
        for s in range(1, n):
            total = total + ar[a, s, lo:hi]
        return total * (1.0 / width)

    def arrive(j):
        m = partners[j]
        if j == 0:
            own[1].wait()
        else:
            x_copy(m, m).wait_recv()

        inv[0, m] = lax.rsqrt(stat[m] * (1.0 / width) + 1e-6)
        states = [xin[m, :, b * LANES:(b + 1) * LANES].T for b in range(blocks)]
        for b in range(blocks):
            xs[0, m, b * LANES:(b + 1) * LANES, :] = states[b]
        fwd(0, m, True, states)

    def arrive_c(j):
        p = partners[j]
        if j == 0:
            own[2].wait()
        else:
            c_copy(p, p, 0).wait_recv()
            c_copy(p, p, 1).wait_recv()

    def chain_of(j):
        return lax.rem(partners[j] + n - TICKS % n, n)

    def turn_c(j):
        turned = [cin[partners[j], :, b * LANES:(b + 1) * LANES].T for b in range(blocks)]
        for b in range(blocks):
            grads[TICKS - 1, order[j], b * LANES:(b + 1) * LANES, :] = turned[b]
        return turned

    def turn_early(lo, hi):
        for j in range(lo, hi):
            arrive_c(j)
        for j in range(lo, hi):
            turn_c(j)

    for j in range(n):
        arrive(j)
    share(0, 0)
    share(0, 1)
    c_send_units(first_cut, second_cut)
    turn_early(0, n // 4)
    for k in range(1, TICKS):
        for h, (lo, hi) in enumerate(halves):
            inv[k, lo:hi] = lax.rsqrt(reduced(k - 1, h) + 1e-6)
            each(lambda m: fwd(k, m, k + 1 < TICKS), lo, hi)
            if k + 1 < TICKS:
                share(k, h)
        if k == 1:
            c_send_units(second_cut, len(units))
            each(response)
            turn_early(n // 4, n // 2)

    def start_back(j, turned=None):
        m, v = chain_of(j), order[j]
        k = TICKS - 1
        l = lax.rem(m + k, n)
        earlier = lax.rem(m + k - 1, n)
        factor = inv[k, m]
        sums = jnp.zeros((1, tok), F32)
        ahead = jnp.zeros((1, tok), F32)
        for group in groups:
            gs = [grads[k, v, span(b)[0], :] if turned is None else turned[b] for b in group]
            hs = []
            for b, g, dprob in zip(group, gs, products(vd, l, group, gs)):
                at, rows = span(b)
                p = probs[k, m, rows, :].reshape(per, src, tok)
                d = softmax_back(p, dprob).astype(BF16)
                ds[k, v, rows, :] = d
                sums = sums + jnp.sum(d.astype(F32) * raws[k, m, rows, :], axis=0, keepdims=True)
                h = g.astype(F32) + factor * (gt[l, at, :] * nn(kdt[l, b], d))
                wide[v, at, :] = h
                hs.append(h.astype(BF16))
            for b, dprob in zip(group, products(vd, earlier, group, hs)):
                _, rows = span(b)
                p = probs[k - 1, m, rows, :].reshape(per, src, tok)
                e = softmax_back(p, dprob)
                e1[v, rows, :] = e
                ahead = ahead + jnp.sum(e * raws[k - 1, m, rows, :], axis=0, keepdims=True)
        return m, sums, ahead

    def keep(rows_of):
        for m, sums, ahead in rows_of:
            br[0, me, m] = sums
            br[1, me, m] = ahead

    def picked(r):
        out = r[:src]
        for i in range(1, per):
            out = jnp.where(sides[i], r[i * src:(i + 1) * src], out)
        return out

    spot = [across((m + TICKS) % n) for m in range(n)]

    def steps(left, right, l):
        out = []
        for group in groups:
            rows = slice(group[0] * brow, (group[-1] + 1) * brow)
            at = slice(group[0] * LANES, (group[-1] + 1) * LANES)
            r = nt(left(l, rows), right(l, at))
            for i in range(len(group)):
                out.append(picked(r[i * brow:(i + 1) * brow, i * LANES:(i + 1) * LANES]))
        return jnp.concatenate(out, axis=1)

    def of_chain(ref):
        return lambda l, rows: ref[2, (l - 2) % n, rows, :]

    def of_spot(ref):
        return lambda l, rows: ref[2, spot[(l - 2) % n], rows, :]

    def pair_of_chain(ref):
        return lambda l, rows: jnp.concatenate(
            [ref[1, (l - 1) % n, rows, :], ref[0, l, rows, :]], axis=1)

    def pair_of_spot(ref):
        return lambda l, rows: jnp.concatenate(
            [ref[1, spot[(l - 1) % n], rows, :], ref[0, spot[l], rows, :]], axis=1)

    def mean_of(a, m):
        total = br[a, 0, m]
        for j in range(1, n):
            total = total + br[a, j, m]
        return total * (1.0 / width)

    def finish_back(j):
        m, v = chain_of(j), order[j]
        l1 = lax.rem(m + 1, n)
        late, early = inv[2, m], inv[1, m]
        c = late * late * mean_of(0, m)
        mean = mean_of(1, m) - c * mean_of(2, m)
        for group in singles:
            gs = []
            for b in group:
                at, rows = span(b)
                g = (wide[v, at, :] - c * xs[2, m, at, :].astype(F32)).astype(BF16)
                grads[1, v, at, :] = g
                d = (e1[v, rows, :] - c * e2[m, rows, :]).astype(BF16)
                ds[1, v, rows, :] = d
                u = xs[1, m, at, :].astype(F32) * early
                g = g.astype(F32) + early * (gt[l1, at, :] * nn(kdt[l1, b], d) - u * mean)
                g = g.astype(BF16)
                grads[0, v, at, :] = g
                gs.append(g)
            for b, dprob in zip(group, products(vd, m, group, gs)):
                _, rows = span(b)
                p = probs[0, m, rows, :].reshape(per, src, tok)
                ds[0, v, rows, :] = softmax_back(p, dprob).astype(BF16)

    keep([start_back(j) for j in range(n // 2)])
    for lo, hi in [(j, j + 2) for j in range(n // 2, n - 2, 2)] + [(n - 2, n - 1), (n - 1, n)]:
        for j in range(lo, hi):
            arrive_c(j)
        turned = [turn_c(j) for j in range(lo, hi)]
        keep([start_back(j, turned[j - lo]) for j in range(lo, hi)])
    peers(lambda p: br_copy(p, me).start())
    for l in range(n):
        ktot[l] = steps(of_spot(ds), of_chain(qs), l)
    for l in range(n):
        vtot[l] = steps(of_chain(plow), of_spot(grads), l)
    peers(lambda p: br_copy(p, p).wait_recv())
    for j in range(n):
        finish_back(j)

    def last(l):
        total = ktot[l] + steps(pair_of_spot(ds), pair_of_chain(qs), l)
        kout_ref[l] = total.astype(BF16)
        gsend[l] = jnp.sum(total * k_ref[l].astype(F32), axis=0, keepdims=True) / gin[l]

    for l in range(n):
        last(l)
    own_gain = pltpu.make_async_copy(gsend.at[me], gdp.at[doc, me], dp_recv)
    others(lambda q, p: dp_copy(q, p, doc, me).start())
    own_gain.start()

    def finish(l):
        vout_ref[l] = (vtot[l] + steps(pair_of_chain(plow), pair_of_spot(grads), l)).astype(BF16)

    for l in range(n):
        finish(l)

    def drain(p):
        x_copy(p, me).wait_send()
        c_copy(p, me, 0).wait_send()
        c_copy(p, me, 1).wait_send()
        g_copy(p, me).wait_send()
        st_copy(p, me).wait_send()
        br_copy(p, me).wait_send()
        for a in range(TICKS - 1):
            for h in range(2):
                ar_copy(a, h, p, me).wait_send()

    peers(drain)
    pltpu.make_async_copy(gdp, gdp, dp_recv).wait()
    for d in range(ndp - 1):
        pltpu.make_async_copy(gdp.at[d], gdp.at[d], dp_send).wait()
    pltpu.make_async_copy(gdp.at[0, 1:], gdp.at[0, 1:], dp_send).wait()
    for s in range(n):
        out = gdp[0, s]
        for d in range(1, ndp):
            out = out + gdp[d, s]
        gout_ref[:, s * cols:(s + 1) * cols] = out


def store(keys, values, gains, kout, vout, gout, done):
    copies = [
        pltpu.make_async_copy(keys, kout.at[0], done.at[0]),
        pltpu.make_async_copy(values, vout.at[0], done.at[1]),
        pltpu.make_async_copy(gains, gout, done.at[2]),
    ]
    for copy in copies:
        copy.start()
    for copy in copies:
        copy.wait()


def on_device(inputs, key_rows, value_rows, query_gain, cotangent):
    n = lax.axis_size("section")
    ndp = lax.axis_size("dp")
    tok, width = inputs.shape[2:]
    src, cols = key_rows.shape[2:]
    blocks = cols // LANES
    brow = LANES // HEAD * src
    rows = blocks * brow
    rounds = TICKS - 1
    vmem = pltpu.VMEM
    sem = pltpu.SemaphoreType.DMA
    scratch = [
        vmem((tok, width), BF16), vmem((n, src, cols), BF16), vmem((n, src, cols), BF16),
        vmem((n, tok, cols), BF16), vmem((n, tok, cols), BF16),
        vmem((n, 1, cols), F32), vmem((n, 1, tok), F32),
        vmem((n, blocks, brow, LANES), BF16), vmem((n, blocks, brow, LANES), BF16),
        vmem((n, blocks, LANES, brow), BF16), vmem((n, blocks, LANES, brow), BF16),
        vmem((n, cols, LANES), F32),
        vmem((TICKS, n, cols, tok), BF16), vmem((TICKS, n, cols, tok), BF16),
        vmem((TICKS, n, rows, tok), F32), vmem((TICKS, n, rows, tok), BF16),
        vmem((TICKS, n, rows, tok), F32),
        vmem((TICKS, n, rows, tok), BF16), vmem((TICKS, n, cols, tok), BF16),
        vmem((n, cols, tok), F32), vmem((n, rows, tok), F32), vmem((n, rows, tok), F32),
        vmem((TICKS, n, 1, tok), F32),
        vmem((rounds, n, n, 1, tok), F32), vmem((3, n, n, 1, tok), F32),
        vmem((n, src, cols), F32), vmem((n, src, cols), F32),
        vmem((n, 1, cols), F32), vmem((ndp, n, 1, cols), F32),
        sem((n,)), sem((n,)), sem((2, n)), sem((2, n)), sem((n,)), sem((n,)), sem((n,)), sem((n,)),
        sem((rounds, 2, n)), sem((rounds, 2, n)), sem((n,)), sem((n,)), sem(()), sem(()), sem((6,)),
    ]
    in_vmem = pl.BlockSpec(memory_space=pltpu.VMEM)
    in_place = pl.BlockSpec(memory_space=pl.ANY)
    unroll = 8
    keys, values, gains = pl.pallas_call(
        functools.partial(kernel, n, ndp, unroll),
        out_shape=(
            vmem((n, src, cols), BF16),
            vmem((n, src, cols), BF16),
            vmem((1, width), F32),
        ),
        in_specs=[in_place] * 5,
        out_specs=(in_vmem, in_vmem, in_vmem),
        scratch_shapes=scratch,
        compiler_params=pltpu.CompilerParams(
            collective_id=0, has_side_effects=True, vmem_limit_bytes=60 * 1024 * 1024),
    )(inputs[0, 0], cotangent[0, 0], key_rows[0], value_rows[0], query_gain)
    return pl.pallas_call(
        store,
        out_shape=(
            jax.ShapeDtypeStruct((1, n, src, cols), BF16),
            jax.ShapeDtypeStruct((1, n, src, cols), BF16),
            jax.ShapeDtypeStruct((1, width), F32),
        ),
        in_specs=[in_place] * 3,
        out_specs=(in_place,) * 3,
        scratch_shapes=[sem((3,))],
        compiler_params=pltpu.CompilerParams(vmem_limit_bytes=1024 * 1024),
    )(keys, values, gains)


def solution(mesh):
    return jax.shard_map(
        on_device,
        mesh=mesh,
        in_specs=(
            P("dp", "section", None, None),
            P("dp", None, None, "section"),
            P("dp", None, None, "section"),
            P("section", None),
            P("dp", "section", None, None),
        ),
        out_specs=(
            P("dp", None, None, "section"),
            P("dp", None, None, "section"),
            P("section", None),
        ),
        check_vma=False,
    )
```

```python
import functools

import jax
import jax.numpy as jnp
from jax import lax
from jax.experimental import pallas as pl
from jax.experimental.pallas import tpu as pltpu
from jax.sharding import PartitionSpec as P

HEAD = 64
TICKS = 3
LANES = 128
MESH = pl.DeviceIdType.MESH
F32 = jnp.float32
BF16 = jnp.bfloat16


def nn(a, b):
    return lax.dot_general(a, b, (((1,), (0,)), ((), ())), preferred_element_type=F32)


def nt(a, b):
    return lax.dot_general(a, b, (((1,), (1,)), ((), ())), preferred_element_type=F32)


def kernel(
    n, ndp, unroll,
    x_ref, ct_ref, k_in, v_in, g_ref,
    kout_ref, vout_ref, gout_ref,
    x_own, k_ref, v_ref,
    xin, cin, gin, stat, kd, vd, kdt, vdt, gt, xs, qs, probs, plow, raws, ds, grads,
    wide, e1, e2, a1, a2, d1, d2, d3, ce, inv, ar, br, ktot, gsend, gdp,
    x_send, x_recv, c_send, c_recv, g_send, g_recv, st_send, st_recv,
    ar_send, ar_recv, br_send, br_recv, dp_send, dp_recv, loc,
):
    me = lax.axis_index("section")
    doc = lax.axis_index("dp")
    tok, width = x_ref.shape
    src, cols = k_in.shape[1], k_in.shape[2]
    blocks = cols // LANES
    per = LANES // HEAD
    brow = per * src
    scale = HEAD ** (-0.5)

    share_of = 2 if blocks % 2 == 0 else 1
    groups = [tuple(range(b, b + share_of)) for b in range(0, blocks, share_of)]

    singles = [(b,) for b in range(blocks)]

    def span(b):
        return slice(b * LANES, (b + 1) * LANES), slice(b * brow, (b + 1) * brow)

    def products(table, l, group, rights):
        left = jnp.concatenate([table[l, b] for b in group], axis=0)
        out = nn(left, jnp.concatenate(rights, axis=1))
        return [out[i * brow:(i + 1) * brow, i * tok:(i + 1) * tok] for i in range(len(group))]

    def partner(j):
        p = me
        for b in range(n.bit_length() - 1):
            if (j >> b) & 1:
                p = p + (1 << b) - (2 << b) * lax.rem(lax.div(me, 1 << b), 2)
        return p

    order = sorted(range(n), key=lambda j: ((j >> 1).bit_count(), j & 1, j))
    partners = [partner(j) for j in order]

    def across(p):
        v = 0
        for b in range(n.bit_length() - 1):
            v = v + (1 << b) * lax.rem(lax.div(me, 1 << b) + lax.div(p, 1 << b), 2)
        return v

    def peers(body, first=1, last=n):
        for p in partners[first:last]:
            body(p)

    def each(body, first=0, last=n, u=None):
        def step(m, c):
            body(m)
            return c
        lax.fori_loop(first, last, step, 0, unroll=u or min(unroll, last - first))

    half = n // 2
    halves = ((0, half), (half, n))

    def to(p, source, target, send, recv):
        return pltpu.make_async_remote_copy(
            src_ref=source, dst_ref=target, send_sem=send, recv_sem=recv,
            device_id={"section": p}, device_id_type=MESH)

    def others(body):
        def step(j, c):
            place = lax.rem(doc * n + me + j, n * ndp)
            body(lax.div(place, n), lax.rem(place, n))
            return c
        lax.fori_loop(1, n * ndp, step, 0)

    def cut(ref, p):
        return ref.at[:, pl.ds(pl.multiple_of(p * cols, LANES), cols)]

    def x_copy(p, slot):
        return to(p, cut(x_ref, p), xin.at[slot], x_send.at[p], x_recv.at[slot])

    def c_copy(p, slot, part):
        rows = pl.ds(part * (tok // 2), tok // 2)
        source = ct_ref.at[rows, pl.ds(pl.multiple_of(p * cols, LANES), cols)]
        return to(p, source, cin.at[slot, rows], c_send.at[part, p], c_recv.at[part, slot])

    units = [(1, 0), (1, 1)]
    for j in range(2, n - 2, 2):
        units += [(j, 0), (j + 1, 0), (j, 1), (j + 1, 1)]
    units += [(j, part) for j in (n - 2, n - 1) for part in (0, 1)]

    def c_send_units(lo, hi):
        for j, part in units[lo:hi]:
            c_copy(partners[j], me, part).start()

    def g_copy(p, slot):
        return to(p, cut(g_ref, p), gin.at[slot], g_send.at[p], g_recv.at[slot])

    def st_copy(p, slot):
        return to(p, stat.at[me], stat.at[slot], st_send.at[p], st_recv.at[slot])

    def ar_copy(a, h, p, slot):
        lo, hi = halves[h]
        return to(p, ar.at[a, me, lo:hi], ar.at[a, slot, lo:hi], ar_send.at[a, h, p], ar_recv.at[a, h, slot])

    def br_copy(p, slot):
        return to(p, br.at[:, me], br.at[:, slot], br_send.at[p], br_recv.at[slot])

    def share(a, h):
        peers(lambda p: ar_copy(a, h, p, me).start())

    def dp_copy(q, p, from_doc, slot):
        return pltpu.make_async_remote_copy(
            src_ref=gsend.at[p], dst_ref=gdp.at[from_doc, slot],
            send_sem=dp_send, recv_sem=dp_recv,
            device_id={"dp": q, "section": p}, device_id_type=MESH)

    barrier = pltpu.get_barrier_semaphore()
    others(lambda q, p: pl.semaphore_signal(
        barrier, inc=1, device_id={"dp": q, "section": p}, device_id_type=MESH))

    own = [
        pltpu.make_async_copy(cut(g_ref, me), gin.at[me], loc.at[0]),
        pltpu.make_async_copy(cut(x_ref, me), xin.at[me], loc.at[1]),
        pltpu.make_async_copy(cut(ct_ref, me), cin.at[me], loc.at[2]),
        pltpu.make_async_copy(x_ref, x_own, loc.at[3]),
        pltpu.make_async_copy(k_in, k_ref, loc.at[4]),
        pltpu.make_async_copy(v_in, v_ref, loc.at[5]),
    ]
    for i in (3, 4, 5, 0, 1, 2):
        own[i].start()

    pl.semaphore_wait(barrier, n * ndp - 1)

    peers(lambda p: g_copy(p, me).start())
    peers(lambda p: x_copy(p, me).start(), 1, n // 2)
    own[3].wait()
    total = jnp.zeros((tok, LANES), F32)
    for b in range(width // LANES):
        part = x_own[:, b * LANES:(b + 1) * LANES].astype(F32)
        total = total + part * part
    stat[me] = jnp.sum(total.T, axis=0, keepdims=True)
    peers(lambda p: st_copy(p, me).start())
    peers(lambda p: x_copy(p, me).start(), n // 2)
    first_cut, second_cut = n - 2, n + 3
    c_send_units(0, first_cut)
    own[4].wait()
    own[5].wait()

    lane = lax.broadcasted_iota(jnp.int32, (src, LANES), 1)
    sides = [jnp.logical_and(lane >= i * HEAD, lane < (i + 1) * HEAD) for i in range(per)]

    def spread(l):
        for source, plain, turned in ((k_ref, kd, kdt), (v_ref, vd, vdt)):
            rows = source[l].astype(F32)
            for b in range(blocks):
                piece = rows[:, b * LANES:(b + 1) * LANES]
                both = jnp.concatenate([jnp.where(s, piece, 0.0) for s in sides], axis=0)
                plain[l, b] = both.astype(BF16)
                turned[l, b] = both.T.astype(BF16)

    each(spread, u=2)

    own[0].wait()
    peers(lambda p: g_copy(p, p).wait_recv())

    def turn_gain(l):
        for b in range(blocks):
            row = gin[l, :, b * LANES:(b + 1) * LANES]
            gt[l, b * LANES:(b + 1) * LANES, :] = jnp.broadcast_to(row, (LANES, LANES)).T

    each(turn_gain, u=2)
    peers(lambda p: st_copy(p, p).wait_recv())

    def softmax_back(p, dprob):
        dprob = dprob.reshape(per, src, tok)
        mean = jnp.sum(p * dprob, axis=1, keepdims=True)
        return (p * (dprob - mean) * scale).reshape(brow, tok)

    def fwd(k, m, more, states=None):
        l = lax.rem(m + k, n)
        factor = inv[k, m]
        pieces = []
        sums = jnp.zeros((1, tok), F32)
        for group in singles:
            xfs, queries = [], []
            for b in group:
                at, _ = span(b)
                xf = (xs[k, m, at, :] if states is None else states[b]).astype(F32)
                q = (xf * factor * gt[l, at, :]).astype(BF16)
                qs[k, m, at, :] = q
                xfs.append(xf)
                queries.append(q)
            scores = products(kd, l, group, queries)
            for b, xf, raw in zip(group, xfs, scores):
                at, rows = span(b)
                raws[k, m, rows, :] = raw
                s3 = raw.reshape(per, src, tok) * scale
                w = jnp.exp(s3 - jnp.max(s3, axis=1, keepdims=True))
                p = w * (1.0 / jnp.sum(w, axis=1, keepdims=True))
                p = p.reshape(brow, tok)
                probs[k, m, rows, :] = p
                low = p.astype(BF16)
                plow[k, m, rows, :] = low
                if more:
                    y = (xf + nn(vdt[l, b], low)).astype(BF16)
                    xs[k + 1, m, at, :] = y
                    yf = y.astype(F32)
                    sums = sums + jnp.sum(yf * yf, axis=0, keepdims=True)
        if more:
            ar[k, me, m] = sums

    def response_0(m):
        for group in groups:
            out = products(vd, m, group, [xs[1, m, span(b)[0], :] for b in group])
            for b, dprob in zip(group, out):
                _, rows = span(b)
                p = probs[0, m, rows, :].reshape(per, src, tok)
                d3[m, rows, :] = softmax_back(p, dprob)

    def response(m):
        l1 = lax.rem(m + 1, n)
        early = inv[1, m]
        sums = jnp.zeros((1, tok), F32)
        for group in groups:
            states = [xs[2, m, span(b)[0], :] for b in group]
            hs = []
            for b, x, dprob in zip(group, states, products(vd, l1, group, states)):
                at, rows = span(b)
                e = softmax_back(probs[1, m, rows, :].reshape(per, src, tok), dprob)
                e2[m, rows, :] = e
                sums = sums + jnp.sum(e * raws[1, m, rows, :], axis=0, keepdims=True)
                a = gt[l1, at, :] * nn(kdt[l1, b], e.astype(BF16))
                a2[m, at, :] = a
                hs.append((x.astype(F32) + early * a).astype(BF16))
            for b, dprob in zip(group, products(vd, m, group, hs)):
                _, rows = span(b)
                d2[m, rows, :] = softmax_back(probs[0, m, rows, :].reshape(per, src, tok), dprob)
        br[2, me, m] = sums

    def reduced(a, h):
        lo, hi = halves[h]
        peers(lambda p: ar_copy(a, h, p, p).wait_recv())
        total = ar[a, 0, lo:hi]
        for s in range(1, n):
            total = total + ar[a, s, lo:hi]
        return total * (1.0 / width)

    def arrive(j):
        m = partners[j]
        if j == 0:
            own[1].wait()
        else:
            x_copy(m, m).wait_recv()

        inv[0, m] = lax.rsqrt(stat[m] * (1.0 / width) + 1e-6)
        states = [xin[m, :, b * LANES:(b + 1) * LANES].T for b in range(blocks)]
        for b in range(blocks):
            xs[0, m, b * LANES:(b + 1) * LANES, :] = states[b]
        fwd(0, m, True, states)

    def arrive_c(j):
        p = partners[j]
        if j == 0:
            own[2].wait()
        else:
            c_copy(p, p, 0).wait_recv()
            c_copy(p, p, 1).wait_recv()

    def chain_of(j):
        return lax.rem(partners[j] + n - TICKS % n, n)

    def turn_c(j):
        turned = [cin[partners[j], :, b * LANES:(b + 1) * LANES].T for b in range(blocks)]
        for b in range(blocks):
            grads[TICKS - 1, order[j], b * LANES:(b + 1) * LANES, :] = turned[b]
        return turned

    def turn_early(lo, hi):
        for j in range(lo, hi):
            arrive_c(j)
        for j in range(lo, hi):
            turn_c(j)

    for j in range(n):
        arrive(j)
    share(0, 0)
    share(0, 1)
    c_send_units(first_cut, second_cut)
    turn_early(0, n // 4)
    each(response_0)
    for k in range(1, TICKS):
        for h, (lo, hi) in enumerate(halves):
            inv[k, lo:hi] = lax.rsqrt(reduced(k - 1, h) + 1e-6)
            each(lambda m: fwd(k, m, k + 1 < TICKS), lo, hi)
            if k + 1 < TICKS:
                share(k, h)
        if k == 1:
            c_send_units(second_cut, len(units))
            each(response)
            turn_early(n // 4, n // 2)

    def start_back(j, turned=None):
        m, v = chain_of(j), order[j]
        k = TICKS - 1
        l = lax.rem(m + k, n)
        earlier = lax.rem(m + k - 1, n)
        factor = inv[k, m]
        sums = jnp.zeros((1, tok), F32)
        ahead = jnp.zeros((1, tok), F32)
        for group in groups:
            gs = [grads[k, v, span(b)[0], :] if turned is None else turned[b] for b in group]
            hs = []
            for b, g, dprob in zip(group, gs, products(vd, l, group, gs)):
                at, rows = span(b)
                p = probs[k, m, rows, :].reshape(per, src, tok)
                d = softmax_back(p, dprob).astype(BF16)
                ds[k, v, rows, :] = d
                sums = sums + jnp.sum(d.astype(F32) * raws[k, m, rows, :], axis=0, keepdims=True)
                h = g.astype(F32) + factor * (gt[l, at, :] * nn(kdt[l, b], d))
                wide[v, at, :] = h
                hs.append(h.astype(BF16))
            for b, dprob in zip(group, products(vd, earlier, group, hs)):
                _, rows = span(b)
                p = probs[k - 1, m, rows, :].reshape(per, src, tok)
                e = softmax_back(p, dprob)
                e1[v, rows, :] = e
                ahead = ahead + jnp.sum(e * raws[k - 1, m, rows, :], axis=0, keepdims=True)
        return m, sums, ahead

    def keep(rows_of):
        for m, sums, ahead in rows_of:
            br[0, me, m] = sums
            br[1, me, m] = ahead

    def picked(r):
        out = r[:src]
        for i in range(1, per):
            out = jnp.where(sides[i], r[i * src:(i + 1) * src], out)
        return out

    spot = [across((m + TICKS) % n) for m in range(n)]

    def steps(left, right, l):
        out = []
        for group in groups:
            rows = slice(group[0] * brow, (group[-1] + 1) * brow)
            at = slice(group[0] * LANES, (group[-1] + 1) * LANES)
            r = nt(left(l, rows), right(l, at))
            for i in range(len(group)):
                out.append(picked(r[i * brow:(i + 1) * brow, i * LANES:(i + 1) * LANES]))
        return jnp.concatenate(out, axis=1)

    def of_chain(ref):
        return lambda l, rows: ref[2, (l - 2) % n, rows, :]

    def of_spot(ref):
        return lambda l, rows: ref[2, spot[(l - 2) % n], rows, :]

    def pair_of_chain(ref):
        return lambda l, rows: jnp.concatenate(
            [ref[1, (l - 1) % n, rows, :], ref[0, l, rows, :]], axis=1)

    def pair_of_spot(ref):
        return lambda l, rows: jnp.concatenate(
            [ref[1, spot[(l - 1) % n], rows, :], ref[0, spot[l], rows, :]], axis=1)

    def mean_of(a, m):
        total = br[a, 0, m]
        for j in range(1, n):
            total = total + br[a, j, m]
        return total * (1.0 / width)

    def advance(j):
        m, v = chain_of(j), order[j]
        l1 = lax.rem(m + 1, n)
        early = inv[1, m]
        for group in groups:
            hs = []
            for b in group:
                at, rows = span(b)
                a = gt[l1, at, :] * nn(kdt[l1, b], e1[v, rows, :].astype(BF16))
                a1[v, at, :] = a
                hs.append((wide[v, at, :] + early * a).astype(BF16))
            for b, dprob in zip(group, products(vd, m, group, hs)):
                _, rows = span(b)
                d1[v, rows, :] = softmax_back(probs[0, m, rows, :].reshape(per, src, tok), dprob)

    def finish_back(j):
        m, v = chain_of(j), order[j]
        late, early = inv[2, m], inv[1, m]
        c = late * late * mean_of(0, m)
        e = early * early * (mean_of(1, m) - c * mean_of(2, m))
        ce[0, v] = c
        ce[1, v] = e
        ds[1, v] = (e1[v] - c * e2[m]).astype(BF16)
        ds[0, v] = (d1[v] - c * d2[m] - e * d3[m]).astype(BF16)

    def gradients(j):
        m, v = chain_of(j), order[j]
        early, c, e = inv[1, m], ce[0, v], ce[1, v]
        for b in range(blocks):
            at, _ = span(b)
            g = (wide[v, at, :] - c * xs[2, m, at, :].astype(F32)).astype(BF16)
            grads[1, v, at, :] = g
            step = early * (a1[v, at, :] - c * a2[m, at, :]) - e * xs[1, m, at, :].astype(F32)
            grads[0, v, at, :] = (g.astype(F32) + step).astype(BF16)

    keep([start_back(j) for j in range(n // 2)])
    for lo, hi in [(j, j + 2) for j in range(n // 2, n - 2, 2)] + [(n - 2, n - 1), (n - 1, n)]:
        for j in range(lo, hi):
            arrive_c(j)
        turned = [turn_c(j) for j in range(lo, hi)]
        keep([start_back(j, turned[j - lo]) for j in range(lo, hi)])
    peers(lambda p: br_copy(p, me).start())
    for l in range(n):
        ktot[l] = steps(of_spot(ds), of_chain(qs), l)
    for j in range(n):
        advance(j)
    peers(lambda p: br_copy(p, p).wait_recv())
    for j in range(n):
        finish_back(j)

    def last(l):
        total = ktot[l] + steps(pair_of_spot(ds), pair_of_chain(qs), l)
        kout_ref[l] = total.astype(BF16)
        gsend[l] = jnp.sum(total * k_ref[l].astype(F32), axis=0, keepdims=True) / gin[l]

    for l in range(n):
        last(l)
    own_gain = pltpu.make_async_copy(gsend.at[me], gdp.at[doc, me], dp_recv)
    others(lambda q, p: dp_copy(q, p, doc, me).start())
    own_gain.start()

    def finish(l):
        total = steps(of_chain(plow), of_spot(grads), l)
        total = total + steps(pair_of_chain(plow), pair_of_spot(grads), l)
        vout_ref[l] = total.astype(BF16)

    for j in range(n):
        gradients(j)
    for l in range(n):
        finish(l)

    def drain(p):
        x_copy(p, me).wait_send()
        c_copy(p, me, 0).wait_send()
        c_copy(p, me, 1).wait_send()
        g_copy(p, me).wait_send()
        st_copy(p, me).wait_send()
        br_copy(p, me).wait_send()
        for a in range(TICKS - 1):
            for h in range(2):
                ar_copy(a, h, p, me).wait_send()

    peers(drain)
    pltpu.make_async_copy(gdp, gdp, dp_recv).wait()
    for d in range(ndp - 1):
        pltpu.make_async_copy(gdp.at[d], gdp.at[d], dp_send).wait()
    pltpu.make_async_copy(gdp.at[0, 1:], gdp.at[0, 1:], dp_send).wait()
    for s in range(n):
        out = gdp[0, s]
        for d in range(1, ndp):
            out = out + gdp[d, s]
        gout_ref[:, s * cols:(s + 1) * cols] = out


def store(keys, values, gains, kout, vout, gout, done):
    copies = [
        pltpu.make_async_copy(keys, kout.at[0], done.at[0]),
        pltpu.make_async_copy(values, vout.at[0], done.at[1]),
        pltpu.make_async_copy(gains, gout, done.at[2]),
    ]
    for copy in copies:
        copy.start()
    for copy in copies:
        copy.wait()


def on_device(inputs, key_rows, value_rows, query_gain, cotangent):
    n = lax.axis_size("section")
    ndp = lax.axis_size("dp")
    tok, width = inputs.shape[2:]
    src, cols = key_rows.shape[2:]
    blocks = cols // LANES
    brow = LANES // HEAD * src
    rows = blocks * brow
    rounds = TICKS - 1
    vmem = pltpu.VMEM
    sem = pltpu.SemaphoreType.DMA
    scratch = [
        vmem((tok, width), BF16), vmem((n, src, cols), BF16), vmem((n, src, cols), BF16),
        vmem((n, tok, cols), BF16), vmem((n, tok, cols), BF16),
        vmem((n, 1, cols), F32), vmem((n, 1, tok), F32),
        vmem((n, blocks, brow, LANES), BF16), vmem((n, blocks, brow, LANES), BF16),
        vmem((n, blocks, LANES, brow), BF16), vmem((n, blocks, LANES, brow), BF16),
        vmem((n, cols, LANES), F32),
        vmem((TICKS, n, cols, tok), BF16), vmem((TICKS, n, cols, tok), BF16),
        vmem((TICKS, n, rows, tok), F32), vmem((TICKS, n, rows, tok), BF16),
        vmem((TICKS, n, rows, tok), F32),
        vmem((TICKS, n, rows, tok), BF16), vmem((TICKS, n, cols, tok), BF16),
        vmem((n, cols, tok), F32), vmem((n, rows, tok), F32), vmem((n, rows, tok), F32),
        vmem((n, cols, tok), F32), vmem((n, cols, tok), F32),
        vmem((n, rows, tok), F32), vmem((n, rows, tok), F32), vmem((n, rows, tok), F32),
        vmem((2, n, 1, tok), F32),
        vmem((TICKS, n, 1, tok), F32),
        vmem((rounds, n, n, 1, tok), F32), vmem((3, n, n, 1, tok), F32),
        vmem((n, src, cols), F32),
        vmem((n, 1, cols), F32), vmem((ndp, n, 1, cols), F32),
        sem((n,)), sem((n,)), sem((2, n)), sem((2, n)), sem((n,)), sem((n,)), sem((n,)), sem((n,)),
        sem((rounds, 2, n)), sem((rounds, 2, n)), sem((n,)), sem((n,)), sem(()), sem(()), sem((6,)),
    ]
    in_vmem = pl.BlockSpec(memory_space=pltpu.VMEM)
    in_place = pl.BlockSpec(memory_space=pl.ANY)
    unroll = 8
    keys, values, gains = pl.pallas_call(
        functools.partial(kernel, n, ndp, unroll),
        out_shape=(
            vmem((n, src, cols), BF16),
            vmem((n, src, cols), BF16),
            vmem((1, width), F32),
        ),
        in_specs=[in_place] * 5,
        out_specs=(in_vmem, in_vmem, in_vmem),
        scratch_shapes=scratch,
        compiler_params=pltpu.CompilerParams(
            collective_id=0, has_side_effects=True, vmem_limit_bytes=60 * 1024 * 1024),
    )(inputs[0, 0], cotangent[0, 0], key_rows[0], value_rows[0], query_gain)
    return pl.pallas_call(
        store,
        out_shape=(
            jax.ShapeDtypeStruct((1, n, src, cols), BF16),
            jax.ShapeDtypeStruct((1, n, src, cols), BF16),
            jax.ShapeDtypeStruct((1, width), F32),
        ),
        in_specs=[in_place] * 3,
        out_specs=(in_place,) * 3,
        scratch_shapes=[sem((3,))],
        compiler_params=pltpu.CompilerParams(vmem_limit_bytes=1024 * 1024),
    )(keys, values, gains)


def solution(mesh):
    return jax.shard_map(
        on_device,
        mesh=mesh,
        in_specs=(
            P("dp", "section", None, None),
            P("dp", None, None, "section"),
            P("dp", None, None, "section"),
            P("section", None),
            P("dp", "section", None, None),
        ),
        out_specs=(
            P("dp", None, None, "section"),
            P("dp", None, None, "section"),
            P("section", None),
        ),
        check_vma=False,
    )
```

```python
import functools

import jax
import jax.numpy as jnp
from jax import lax
from jax.experimental import pallas as pl
from jax.experimental.pallas import tpu as pltpu
from jax.sharding import PartitionSpec as P

HEAD = 64
TICKS = 3
LANES = 128
MESH = pl.DeviceIdType.MESH
F32 = jnp.float32
BF16 = jnp.bfloat16


def nn(a, b):
    return lax.dot_general(a, b, (((1,), (0,)), ((), ())), preferred_element_type=F32)


def nt(a, b):
    return lax.dot_general(a, b, (((1,), (1,)), ((), ())), preferred_element_type=F32)


def kernel(
    n, ndp, unroll,
    x_ref, ct_ref, k_in, v_in, g_ref,
    kout_ref, vout_ref, gout_ref,
    x_own, k_ref, v_ref,
    xin, cin, gin, stat, kd, vd, kdt, vdt, gt, xs, qs, probs, plow, raws, ds, grads,
    wide, e1, e2, a1, a2, d1, d2, d3, ce, inv, ar, br, ktot, gsend, gdp,
    x_send, x_recv, c_send, c_recv, g_send, g_recv, st_send, st_recv,
    ar_send, ar_recv, br_send, br_recv, dp_send, dp_recv, loc,
):
    me = lax.axis_index("section")
    doc = lax.axis_index("dp")
    tok, width = x_ref.shape
    src, cols = k_in.shape[1], k_in.shape[2]
    blocks = cols // LANES
    per = LANES // HEAD
    brow = per * src
    scale = HEAD ** (-0.5)

    share_of = 2 if blocks % 2 == 0 else 1
    groups = [tuple(range(b, b + share_of)) for b in range(0, blocks, share_of)]

    singles = [(b,) for b in range(blocks)]

    def span(b):
        return slice(b * LANES, (b + 1) * LANES), slice(b * brow, (b + 1) * brow)

    def products(table, l, group, rights):
        left = jnp.concatenate([table[l, b] for b in group], axis=0)
        out = nn(left, jnp.concatenate(rights, axis=1))
        return [out[i * brow:(i + 1) * brow, i * tok:(i + 1) * tok] for i in range(len(group))]

    def partner(j):
        p = me
        for b in range(n.bit_length() - 1):
            if (j >> b) & 1:
                p = p + (1 << b) - (2 << b) * lax.rem(lax.div(me, 1 << b), 2)
        return p

    order = sorted(range(n), key=lambda j: ((j >> 1).bit_count(), j & 1, j))
    partners = [partner(j) for j in order]

    def across(p):
        v = 0
        for b in range(n.bit_length() - 1):
            v = v + (1 << b) * lax.rem(lax.div(me, 1 << b) + lax.div(p, 1 << b), 2)
        return v

    def peers(body, first=1, last=n):
        for p in partners[first:last]:
            body(p)

    def each(body, first=0, last=n, u=None):
        def step(m, c):
            body(m)
            return c
        lax.fori_loop(first, last, step, 0, unroll=u or min(unroll, last - first))

    half = n // 2
    halves = ((0, half), (half, n))

    def to(p, source, target, send, recv):
        return pltpu.make_async_remote_copy(
            src_ref=source, dst_ref=target, send_sem=send, recv_sem=recv,
            device_id={"section": p}, device_id_type=MESH)

    def documents(body):
        def step(d, c):
            body(lax.rem(doc + d, ndp))
            return c
        lax.fori_loop(1, ndp, step, 0, unroll=ndp - 1 if ndp <= 4 else 1)

    def others(body):
        def elsewhere(q):
            for p in range(n):
                body(q, p)
        documents(elsewhere)
        for p in partners[1:]:
            body(doc, p)

    def cut(ref, p):
        return ref.at[:, pl.ds(pl.multiple_of(p * cols, LANES), cols)]

    def x_copy(p, slot):
        return to(p, cut(x_ref, p), xin.at[slot], x_send.at[p], x_recv.at[slot])

    def c_copy(p, slot, part):
        rows = pl.ds(part * (tok // 2), tok // 2)
        source = ct_ref.at[rows, pl.ds(pl.multiple_of(p * cols, LANES), cols)]
        return to(p, source, cin.at[slot, rows], c_send.at[part, p], c_recv.at[part, slot])

    units = [(1, 0), (1, 1)]
    for j in range(2, n - 2, 2):
        units += [(j, 0), (j + 1, 0), (j, 1), (j + 1, 1)]
    units += [(j, part) for j in (n - 2, n - 1) for part in (0, 1)]

    def c_send_units(lo, hi):
        for j, part in units[lo:hi]:
            c_copy(partners[j], me, part).start()

    def g_copy(p, slot):
        return to(p, cut(g_ref, p), gin.at[slot], g_send.at[p], g_recv.at[slot])

    def st_copy(p, slot):
        return to(p, stat.at[me], stat.at[slot], st_send.at[p], st_recv.at[slot])

    def ar_copy(a, h, p, slot):
        lo, hi = halves[h]
        return to(p, ar.at[a, me, lo:hi], ar.at[a, slot, lo:hi], ar_send.at[a, h, p], ar_recv.at[a, h, slot])

    def br_copy(p, slot):
        return to(p, br.at[:, me], br.at[:, slot], br_send.at[p], br_recv.at[slot])

    def share(a, h):
        peers(lambda p: ar_copy(a, h, p, me).start())

    def dp_copy(q, p, from_doc, slot):
        return pltpu.make_async_remote_copy(
            src_ref=gsend.at[p], dst_ref=gdp.at[from_doc, slot],
            send_sem=dp_send, recv_sem=dp_recv,
            device_id={"dp": q, "section": p}, device_id_type=MESH)

    barrier = pltpu.get_barrier_semaphore()
    others(lambda q, p: pl.semaphore_signal(
        barrier, inc=1, device_id={"dp": q, "section": p}, device_id_type=MESH))

    own = [
        pltpu.make_async_copy(cut(g_ref, me), gin.at[me], loc.at[0]),
        pltpu.make_async_copy(cut(x_ref, me), xin.at[me], loc.at[1]),
        pltpu.make_async_copy(cut(ct_ref, me), cin.at[me], loc.at[2]),
        pltpu.make_async_copy(x_ref, x_own, loc.at[3]),
        pltpu.make_async_copy(k_in, k_ref, loc.at[4]),
        pltpu.make_async_copy(v_in, v_ref, loc.at[5]),
    ]
    for i in (3, 4, 5, 0, 1, 2):
        own[i].start()

    pl.semaphore_wait(barrier, n * ndp - 1)

    peers(lambda p: g_copy(p, me).start())
    peers(lambda p: x_copy(p, me).start(), 1, n // 2)
    own[3].wait()
    total = jnp.zeros((tok, LANES), F32)
    for b in range(width // LANES):
        part = x_own[:, b * LANES:(b + 1) * LANES].astype(F32)
        total = total + part * part
    stat[me] = jnp.sum(total.T, axis=0, keepdims=True)
    peers(lambda p: st_copy(p, me).start())
    peers(lambda p: x_copy(p, me).start(), n // 2)
    first_cut, second_cut = n - 2, n + 3
    c_send_units(0, first_cut)
    own[4].wait()
    own[5].wait()

    lane = lax.broadcasted_iota(jnp.int32, (src, LANES), 1)
    sides = [jnp.logical_and(lane >= i * HEAD, lane < (i + 1) * HEAD) for i in range(per)]

    def spread(l):
        for source, plain, turned in ((k_ref, kd, kdt), (v_ref, vd, vdt)):
            rows = source[l].astype(F32)
            for b in range(blocks):
                piece = rows[:, b * LANES:(b + 1) * LANES]
                both = jnp.concatenate([jnp.where(s, piece, 0.0) for s in sides], axis=0)
                plain[l, b] = both.astype(BF16)
                turned[l, b] = both.T.astype(BF16)

    each(spread, u=2)

    own[0].wait()
    peers(lambda p: g_copy(p, p).wait_recv())

    def turn_gain(l):
        for b in range(blocks):
            row = gin[l, :, b * LANES:(b + 1) * LANES]
            gt[l, b * LANES:(b + 1) * LANES, :] = jnp.broadcast_to(row, (LANES, LANES)).T

    each(turn_gain, u=2)
    peers(lambda p: st_copy(p, p).wait_recv())

    def softmax_back(p, dprob):
        dprob = dprob.reshape(per, src, tok)
        mean = jnp.sum(p * dprob, axis=1, keepdims=True)
        return (p * (dprob - mean) * scale).reshape(brow, tok)

    def fwd(k, m, more, states=None):
        l = lax.rem(m + k, n)
        factor = inv[k, m]
        pieces = []
        sums = jnp.zeros((1, tok), F32)
        for group in singles:
            xfs, queries = [], []
            for b in group:
                at, _ = span(b)
                xf = (xs[k, m, at, :] if states is None else states[b]).astype(F32)
                q = (xf * factor * gt[l, at, :]).astype(BF16)
                qs[k, m, at, :] = q
                xfs.append(xf)
                queries.append(q)
            scores = products(kd, l, group, queries)
            for b, xf, raw in zip(group, xfs, scores):
                at, rows = span(b)
                raws[k, m, rows, :] = raw
                s3 = raw.reshape(per, src, tok) * scale
                w = jnp.exp(s3 - jnp.max(s3, axis=1, keepdims=True))
                p = w * (1.0 / jnp.sum(w, axis=1, keepdims=True))
                p = p.reshape(brow, tok)
                probs[k, m, rows, :] = p
                low = p.astype(BF16)
                plow[k, m, rows, :] = low
                if more:
                    y = (xf + nn(vdt[l, b], low)).astype(BF16)
                    xs[k + 1, m, at, :] = y
                    yf = y.astype(F32)
                    sums = sums + jnp.sum(yf * yf, axis=0, keepdims=True)
        if more:
            ar[k, me, m] = sums

    def response_0(m):
        for group in groups:
            out = products(vd, m, group, [xs[1, m, span(b)[0], :] for b in group])
            for b, dprob in zip(group, out):
                _, rows = span(b)
                p = probs[0, m, rows, :].reshape(per, src, tok)
                d3[m, rows, :] = softmax_back(p, dprob)

    def response(m):
        l1 = lax.rem(m + 1, n)
        early = inv[1, m]
        sums = jnp.zeros((1, tok), F32)
        for group in groups:
            states = [xs[2, m, span(b)[0], :] for b in group]
            hs = []
            for b, x, dprob in zip(group, states, products(vd, l1, group, states)):
                at, rows = span(b)
                e = softmax_back(probs[1, m, rows, :].reshape(per, src, tok), dprob)
                e2[m, rows, :] = e
                sums = sums + jnp.sum(e * raws[1, m, rows, :], axis=0, keepdims=True)
                a = gt[l1, at, :] * nn(kdt[l1, b], e.astype(BF16))
                a2[m, at, :] = a
                hs.append((x.astype(F32) + early * a).astype(BF16))
            for b, dprob in zip(group, products(vd, m, group, hs)):
                _, rows = span(b)
                d2[m, rows, :] = softmax_back(probs[0, m, rows, :].reshape(per, src, tok), dprob)
        br[2, me, m] = sums

    def reduced(a, h):
        lo, hi = halves[h]
        peers(lambda p: ar_copy(a, h, p, p).wait_recv())
        total = ar[a, 0, lo:hi]
        for s in range(1, n):
            total = total + ar[a, s, lo:hi]
        return total * (1.0 / width)

    def arrive(j):
        m = partners[j]
        if j == 0:
            own[1].wait()
        else:
            x_copy(m, m).wait_recv()

        inv[0, m] = lax.rsqrt(stat[m] * (1.0 / width) + 1e-6)
        states = [xin[m, :, b * LANES:(b + 1) * LANES].T for b in range(blocks)]
        for b in range(blocks):
            xs[0, m, b * LANES:(b + 1) * LANES, :] = states[b]
        fwd(0, m, True, states)

    def arrive_c(j):
        p = partners[j]
        if j == 0:
            own[2].wait()
        else:
            c_copy(p, p, 0).wait_recv()
            c_copy(p, p, 1).wait_recv()

    def chain_of(j):
        return lax.rem(partners[j] + n - TICKS % n, n)

    def turn_c(j):
        turned = [cin[partners[j], :, b * LANES:(b + 1) * LANES].T for b in range(blocks)]
        for b in range(blocks):
            grads[TICKS - 1, order[j], b * LANES:(b + 1) * LANES, :] = turned[b]
        return turned

    def turn_early(lo, hi):
        for j in range(lo, hi):
            arrive_c(j)
        for j in range(lo, hi):
            turn_c(j)

    for j in range(n):
        arrive(j)
    share(0, 0)
    share(0, 1)
    c_send_units(first_cut, second_cut)
    turn_early(0, n // 4)
    each(response_0)
    for k in range(1, TICKS):
        for h, (lo, hi) in enumerate(halves):
            inv[k, lo:hi] = lax.rsqrt(reduced(k - 1, h) + 1e-6)
            each(lambda m: fwd(k, m, k + 1 < TICKS), lo, hi)
            if k + 1 < TICKS:
                share(k, h)
        if k == 1:
            c_send_units(second_cut, len(units))
            each(response)
            turn_early(n // 4, n // 2)

    def start_back(j, turned=None):
        m, v = chain_of(j), order[j]
        k = TICKS - 1
        l = lax.rem(m + k, n)
        earlier = lax.rem(m + k - 1, n)
        factor = inv[k, m]
        sums = jnp.zeros((1, tok), F32)
        ahead = jnp.zeros((1, tok), F32)
        for group in groups:
            gs = [grads[k, v, span(b)[0], :] if turned is None else turned[b] for b in group]
            hs = []
            for b, g, dprob in zip(group, gs, products(vd, l, group, gs)):
                at, rows = span(b)
                p = probs[k, m, rows, :].reshape(per, src, tok)
                d = softmax_back(p, dprob).astype(BF16)
                ds[k, v, rows, :] = d
                sums = sums + jnp.sum(d.astype(F32) * raws[k, m, rows, :], axis=0, keepdims=True)
                h = g.astype(F32) + factor * (gt[l, at, :] * nn(kdt[l, b], d))
                wide[v, at, :] = h
                hs.append(h.astype(BF16))
            for b, dprob in zip(group, products(vd, earlier, group, hs)):
                _, rows = span(b)
                p = probs[k - 1, m, rows, :].reshape(per, src, tok)
                e = softmax_back(p, dprob)
                e1[v, rows, :] = e
                ahead = ahead + jnp.sum(e * raws[k - 1, m, rows, :], axis=0, keepdims=True)
        return m, sums, ahead

    def keep(rows_of):
        for m, sums, ahead in rows_of:
            br[0, me, m] = sums
            br[1, me, m] = ahead

    def picked(r):
        out = r[:src]
        for i in range(1, per):
            out = jnp.where(sides[i], r[i * src:(i + 1) * src], out)
        return out

    spot = [across((m + TICKS) % n) for m in range(n)]

    def steps(left, right, l):
        out = []
        for group in groups:
            rows = slice(group[0] * brow, (group[-1] + 1) * brow)
            at = slice(group[0] * LANES, (group[-1] + 1) * LANES)
            r = nt(left(l, rows), right(l, at))
            for i in range(len(group)):
                out.append(picked(r[i * brow:(i + 1) * brow, i * LANES:(i + 1) * LANES]))
        return jnp.concatenate(out, axis=1)

    def of_chain(ref):
        return lambda l, rows: ref[2, (l - 2) % n, rows, :]

    def of_spot(ref):
        return lambda l, rows: ref[2, spot[(l - 2) % n], rows, :]

    def pair_of_chain(ref):
        return lambda l, rows: jnp.concatenate(
            [ref[1, (l - 1) % n, rows, :], ref[0, l, rows, :]], axis=1)

    def pair_of_spot(ref):
        return lambda l, rows: jnp.concatenate(
            [ref[1, spot[(l - 1) % n], rows, :], ref[0, spot[l], rows, :]], axis=1)

    def mean_of(a, m):
        total = br[a, 0, m]
        for j in range(1, n):
            total = total + br[a, j, m]
        return total * (1.0 / width)

    def advance(j):
        m, v = chain_of(j), order[j]
        l1 = lax.rem(m + 1, n)
        early = inv[1, m]
        for group in groups:
            hs = []
            for b in group:
                at, rows = span(b)
                a = gt[l1, at, :] * nn(kdt[l1, b], e1[v, rows, :].astype(BF16))
                a1[v, at, :] = a
                hs.append((wide[v, at, :] + early * a).astype(BF16))
            for b, dprob in zip(group, products(vd, m, group, hs)):
                _, rows = span(b)
                d1[v, rows, :] = softmax_back(probs[0, m, rows, :].reshape(per, src, tok), dprob)

    def finish_back(j):
        m, v = chain_of(j), order[j]
        late, early = inv[2, m], inv[1, m]
        c = late * late * mean_of(0, m)
        e = early * early * (mean_of(1, m) - c * mean_of(2, m))
        ce[0, v] = c
        ce[1, v] = e
        ds[1, v] = (e1[v] - c * e2[m]).astype(BF16)
        ds[0, v] = (d1[v] - c * d2[m] - e * d3[m]).astype(BF16)

    def gradients(j):
        m, v = chain_of(j), order[j]
        early, c, e = inv[1, m], ce[0, v], ce[1, v]
        for b in range(blocks):
            at, _ = span(b)
            g = (wide[v, at, :] - c * xs[2, m, at, :].astype(F32)).astype(BF16)
            grads[1, v, at, :] = g
            step = early * (a1[v, at, :] - c * a2[m, at, :]) - e * xs[1, m, at, :].astype(F32)
            grads[0, v, at, :] = (g.astype(F32) + step).astype(BF16)

    keep([start_back(j) for j in range(n // 2)])
    for lo, hi in [(j, j + 2) for j in range(n // 2, n - 2, 2)] + [(n - 2, n - 1), (n - 1, n)]:
        for j in range(lo, hi):
            arrive_c(j)
        turned = [turn_c(j) for j in range(lo, hi)]
        keep([start_back(j, turned[j - lo]) for j in range(lo, hi)])
    peers(lambda p: br_copy(p, me).start())
    for l in range(n):
        ktot[l] = steps(of_spot(ds), of_chain(qs), l)
    for j in range(n):
        advance(j)
    peers(lambda p: br_copy(p, p).wait_recv())
    for j in range(n):
        finish_back(j)

    def last(l):
        total = ktot[l] + steps(pair_of_spot(ds), pair_of_chain(qs), l)
        kout_ref[l] = total.astype(BF16)
        gsend[l] = jnp.sum(total * k_ref[l].astype(F32), axis=0, keepdims=True) / gin[l]

    for l in range(n):
        last(l)
    own_gain = pltpu.make_async_copy(gsend.at[me], gdp.at[doc, me], dp_recv)
    others(lambda q, p: dp_copy(q, p, doc, me).start())
    own_gain.start()

    def finish(l):
        total = steps(of_chain(plow), of_spot(grads), l)
        total = total + steps(pair_of_chain(plow), pair_of_spot(grads), l)
        vout_ref[l] = total.astype(BF16)

    for j in range(n):
        gradients(j)
    for l in range(n):
        finish(l)

    def drain(p):
        x_copy(p, me).wait_send()
        c_copy(p, me, 0).wait_send()
        c_copy(p, me, 1).wait_send()
        g_copy(p, me).wait_send()
        st_copy(p, me).wait_send()
        br_copy(p, me).wait_send()
        for a in range(TICKS - 1):
            for h in range(2):
                ar_copy(a, h, p, me).wait_send()

    peers(drain)
    pltpu.make_async_copy(gdp, gdp, dp_recv).wait()
    for d in range(ndp - 1):
        pltpu.make_async_copy(gdp.at[d], gdp.at[d], dp_send).wait()
    pltpu.make_async_copy(gdp.at[0, 1:], gdp.at[0, 1:], dp_send).wait()
    for s in range(n):
        out = gdp[0, s]
        for d in range(1, ndp):
            out = out + gdp[d, s]
        gout_ref[:, s * cols:(s + 1) * cols] = out


def store(keys, values, gains, kout, vout, gout, done):
    copies = [
        pltpu.make_async_copy(keys, kout.at[0], done.at[0]),
        pltpu.make_async_copy(values, vout.at[0], done.at[1]),
        pltpu.make_async_copy(gains, gout, done.at[2]),
    ]
    for copy in copies:
        copy.start()
    for copy in copies:
        copy.wait()


def on_device(inputs, key_rows, value_rows, query_gain, cotangent):
    n = lax.axis_size("section")
    ndp = lax.axis_size("dp")
    tok, width = inputs.shape[2:]
    src, cols = key_rows.shape[2:]
    blocks = cols // LANES
    brow = LANES // HEAD * src
    rows = blocks * brow
    rounds = TICKS - 1
    vmem = pltpu.VMEM
    sem = pltpu.SemaphoreType.DMA
    scratch = [
        vmem((tok, width), BF16), vmem((n, src, cols), BF16), vmem((n, src, cols), BF16),
        vmem((n, tok, cols), BF16), vmem((n, tok, cols), BF16),
        vmem((n, 1, cols), F32), vmem((n, 1, tok), F32),
        vmem((n, blocks, brow, LANES), BF16), vmem((n, blocks, brow, LANES), BF16),
        vmem((n, blocks, LANES, brow), BF16), vmem((n, blocks, LANES, brow), BF16),
        vmem((n, cols, LANES), F32),
        vmem((TICKS, n, cols, tok), BF16), vmem((TICKS, n, cols, tok), BF16),
        vmem((TICKS, n, rows, tok), F32), vmem((TICKS, n, rows, tok), BF16),
        vmem((TICKS, n, rows, tok), F32),
        vmem((TICKS, n, rows, tok), BF16), vmem((TICKS, n, cols, tok), BF16),
        vmem((n, cols, tok), F32), vmem((n, rows, tok), F32), vmem((n, rows, tok), F32),
        vmem((n, cols, tok), F32), vmem((n, cols, tok), F32),
        vmem((n, rows, tok), F32), vmem((n, rows, tok), F32), vmem((n, rows, tok), F32),
        vmem((2, n, 1, tok), F32),
        vmem((TICKS, n, 1, tok), F32),
        vmem((rounds, n, n, 1, tok), F32), vmem((3, n, n, 1, tok), F32),
        vmem((n, src, cols), F32),
        vmem((n, 1, cols), F32), vmem((ndp, n, 1, cols), F32),
        sem((n,)), sem((n,)), sem((2, n)), sem((2, n)), sem((n,)), sem((n,)), sem((n,)), sem((n,)),
        sem((rounds, 2, n)), sem((rounds, 2, n)), sem((n,)), sem((n,)), sem(()), sem(()), sem((6,)),
    ]
    in_vmem = pl.BlockSpec(memory_space=pltpu.VMEM)
    in_place = pl.BlockSpec(memory_space=pl.ANY)
    unroll = 8
    keys, values, gains = pl.pallas_call(
        functools.partial(kernel, n, ndp, unroll),
        out_shape=(
            vmem((n, src, cols), BF16),
            vmem((n, src, cols), BF16),
            vmem((1, width), F32),
        ),
        in_specs=[in_place] * 5,
        out_specs=(in_vmem, in_vmem, in_vmem),
        scratch_shapes=scratch,
        compiler_params=pltpu.CompilerParams(
            collective_id=0, has_side_effects=True, vmem_limit_bytes=60 * 1024 * 1024),
    )(inputs[0, 0], cotangent[0, 0], key_rows[0], value_rows[0], query_gain)
    return pl.pallas_call(
        store,
        out_shape=(
            jax.ShapeDtypeStruct((1, n, src, cols), BF16),
            jax.ShapeDtypeStruct((1, n, src, cols), BF16),
            jax.ShapeDtypeStruct((1, width), F32),
        ),
        in_specs=[in_place] * 3,
        out_specs=(in_place,) * 3,
        scratch_shapes=[sem((3,))],
        compiler_params=pltpu.CompilerParams(vmem_limit_bytes=1024 * 1024),
    )(keys, values, gains)


def solution(mesh):
    return jax.shard_map(
        on_device,
        mesh=mesh,
        in_specs=(
            P("dp", "section", None, None),
            P("dp", None, None, "section"),
            P("dp", None, None, "section"),
            P("section", None),
            P("dp", "section", None, None),
        ),
        out_specs=(
            P("dp", None, None, "section"),
            P("dp", None, None, "section"),
            P("section", None),
        ),
        check_vma=False,
    )
```
